32 devices in a mesh: rep: 2 (over x), grp: 4 (over z), tp: 4 (over y, core).
Axes of the slice: x: 2, y: 2, z: 4, core: 2. Of those that a mesh axis runs over, the one named last changes fastest.
Arguments:
- queries: bfloat16 [512, 8192], P(('rep', 'grp'), 'tp'), parts along dimension 0, may hold values from -256 to 256
- newest_key_value: bfloat16 [512, 2, 1024], P(('rep', 'grp')), parts along dimension 0, may hold values from -6 to 6
- kv_pages: bfloat16 [128, 2, 128, 1024], P(('rep', 'grp', 'tp')), parts along dimension 0, may hold values from -8 to 8
- fetch_slots: int32 [8, 16, 2], P('rep', ('grp', 'tp')), parts along dimension 0, may hold values from -1 to 3, as said below
- block_table: int32 [512, 8], P(('rep', 'grp')), parts along dimension 0, may hold values from 0 to 31, as said below
- prefix_len: int32 [512], P(('rep', 'grp')), parts along dimension 0, may hold values from 2 to 1024
- out_weight: bfloat16 [8192, 8192], P('tp'), may hold values from -0.09375 to 0.09375
Outputs:
- attended: bfloat16 [512, 8192], P(('rep', 'grp'), 'tp'), parts along dimension 0
The draws below stay inside these ranges and needn't reach their ends.
There are 2 independent parts, one for each index of `rep`. The reference program is written for one: setup_inputs(seed, part) draws one part's arguments, and reference() takes and returns one part's arrays. A program takes and returns all parts, laid end to end along the dimension named above; an argument that names none is the same for every part. Nothing has to cross between parts.
Inputs may be any that keep to these rules, and one draw needn't show every extreme that they name: `fetch_slots`: entries of one (group, owner device) are distinct pages of that device's storage; each group takes at most 2 pages from one device, and in every draw some group takes exactly 2 from some device; -1 marks an unused entry, and used entries come first. `block_table`: every entry names a used entry of its group's fetch_slots; requests of a group share their first pages to a varying depth.
All inputs are finite; a program needn't handle non-finite values.
Results may differ from the reference program's by a relative error of at most 0.0057.
Values may be sent and summed in bfloat16 or wider, within the bound.
A program may use at most 128 MiB of HBM per device.

```python
import math
import jax
import jax.numpy as jnp
from jax import lax

D = 8192
QUERY_HEADS = 64
KEY_VALUE_HEADS = 8
HEAD_SIZE = 128
PAGE_TOKENS = 128
PAGE_LIST_LENGTH = 8
GROUP_PAGE_LIMIT = 2
REQ_GRP = 64
PAGES_DEV = 4
OWNERS = 16
TOTAL_PAGES = 64
SLOTS = 32
TOTAL_REQUESTS = 256
N_GRP = 4


def fetch_plan(key):
    base = jax.random.fold_in(key, 101)
    hot_owner = jax.random.randint(jax.random.fold_in(base, 1), (OWNERS,), 0, 4) == 0
    counts = jax.random.randint(jax.random.fold_in(base, 2), (N_GRP, OWNERS), 0, GROUP_PAGE_LIMIT + 1)
    counts = jnp.where(hot_owner[None, :], GROUP_PAGE_LIMIT, counts)
    forced = jnp.arange(N_GRP) * 7 % OWNERS
    counts = counts.at[jnp.arange(N_GRP), forced].set(GROUP_PAGE_LIMIT)
    perm_keys = jax.random.split(jax.random.fold_in(base, 3), N_GRP * OWNERS)
    perms = jax.vmap(lambda one_key: jax.random.permutation(one_key, PAGES_DEV)[:GROUP_PAGE_LIMIT])(perm_keys)
    perms = perms.reshape(N_GRP, OWNERS, GROUP_PAGE_LIMIT)
    filled = jnp.arange(GROUP_PAGE_LIMIT)[None, None, :] < counts[..., None]
    slots = jnp.where(filled, perms, -1).astype(jnp.int32)
    return (slots, filled)


def page_table(key):
    slots, filled = fetch_plan(key)
    flags = filled.reshape(N_GRP, SLOTS).astype(jnp.int32)
    order = jnp.argsort(1 - flags, axis=1, stable=True).astype(jnp.int32)
    count = jnp.sum(flags, axis=1)
    base = jax.random.fold_in(key, 202)
    group_of = jnp.arange(TOTAL_REQUESTS) // REQ_GRP
    shared_pick = jax.random.randint(jax.random.fold_in(base, 1), (N_GRP, PAGE_LIST_LENGTH), 0, 1 << 20) % count[:, None]
    own_pick = jax.random.randint(jax.random.fold_in(base, 2), (TOTAL_REQUESTS, PAGE_LIST_LENGTH), 0, 1 << 20) % count[group_of][:, None]
    depth = jax.random.randint(jax.random.fold_in(base, 3), (TOTAL_REQUESTS,), 0, PAGE_LIST_LENGTH + 1)
    pick = jnp.where(jnp.arange(PAGE_LIST_LENGTH)[None, :] < depth[:, None], shared_pick[group_of], own_pick)
    return jnp.take_along_axis(order[group_of], pick, axis=1).astype(jnp.int32)


def key_couples(key):
    first_index = jax.random.normal(jax.random.fold_in(key, 404), (TOTAL_PAGES, 2, KEY_VALUE_HEADS * HEAD_SIZE), jnp.float32)
    return jnp.clip(first_index, -6.0, 6.0)


def draw_fetch_slots(key, part):
    return fetch_plan(key)[0]


def draw_block_table(key, part):
    return page_table(key)


def draw_kv_pages(key, part):
    remaining_rows = jax.random.normal(jax.random.fold_in(key, 505), (TOTAL_PAGES, 2, PAGE_TOKENS, KEY_VALUE_HEADS * HEAD_SIZE), jnp.float32)
    remaining_rows = jnp.clip(remaining_rows, -6.0, 6.0)
    remaining_rows = remaining_rows.at[:, 0, 0:2].set(key_couples(key))
    return remaining_rows.astype(jnp.bfloat16)


def draw_queries(key, part):
    drawn = jax.random.normal(jax.random.fold_in(key, 606), (TOTAL_REQUESTS, QUERY_HEADS * HEAD_SIZE), jnp.float32)
    drawn = jnp.clip(drawn, -6.0, 6.0)
    return drawn.astype(jnp.bfloat16)


def place_ends(values, own_key, least, high):
    index_at = [jax.random.randint(jax.random.fold_in(own_key, axis), (), 0, length) for axis, length in enumerate(values.shape)]
    longest = values.shape.index(max(values.shape))
    neighbour = index_at[:longest] + [(index_at[longest] + 1) % values.shape[longest]] + index_at[longest + 1:]
    return values.at[tuple(index_at)].set(least).at[tuple(neighbour)].set(high)


def strengthened(result, stream_key, source, target, parts, factor):
    owner, partner = [(jnp.arange(result.shape[axis_at]) // (result.shape[axis_at] // parts)).reshape([-1 if axis == axis_at else 1 for axis in range(result.ndim)]) for axis_at in (source, target)]
    chosen = jax.random.permutation(stream_key, parts)[partner]
    strong = (owner == chosen) | (owner == (partner + parts // 2) % parts)
    return jnp.where(strong, factor * result, result)


def level_of(own_key, dims, shards, smallest, largest):
    level, own = 1.0, jax.random.fold_in(own_key, 6)
    for dim, parts in shards:
        steps = jnp.exp(jax.random.uniform(jax.random.fold_in(own, dim), (parts,), jnp.float32, smallest / len(shards), largest / len(shards)))
        level = level * jnp.repeat(steps, dims[dim] // parts).reshape([-1 if axis == dim else 1 for axis in range(len(dims))])
    return level


def gaussian(key, shape, deviation, limit, cuts=(), held_as=jnp.bfloat16):
    values = jax.random.normal(key, shape, jnp.float32) * deviation
    if len(cuts) > 0:
        values = level_of(key, shape, cuts, -0.22, 0.18) * values
    return jnp.clip(values, min=-limit, max=limit).astype(held_as)


def heavy_noise(stream_key, dims, spread, bound, cuts, heavy, kind=jnp.bfloat16):
    entries = spread * jax.random.normal(stream_key, dims, jnp.float32)
    if cuts:
        entries = entries * level_of(stream_key, dims, cuts, -0.22, 0.18)
    return jnp.clip(strengthened(entries, jax.random.fold_in(stream_key, 3), *heavy), -bound, bound).astype(kind)


def setup_inputs(seed: int = 0, part: int = 0) -> dict:
    keys = jax.random.split(jax.random.key(seed), 8)
    part_splits = jax.random.split(jax.random.fold_in(keys[7], part), 8)
    queries = draw_queries(jax.random.fold_in(jax.random.fold_in(keys[7], part), 71), part)
    newest_key_value = gaussian(part_splits[1], (TOTAL_REQUESTS, 2, KEY_VALUE_HEADS * HEAD_SIZE), 1.0, 6.0, ((0, 4),))
    kv_pages = draw_kv_pages(jax.random.fold_in(jax.random.fold_in(keys[7], part), 71), part)
    fetch_slots = draw_fetch_slots(jax.random.fold_in(jax.random.fold_in(keys[7], part), 71), part)
    block_table = draw_block_table(jax.random.fold_in(jax.random.fold_in(keys[7], part), 71), part)
    prefix_len = place_ends(jax.random.randint(part_splits[5], (TOTAL_REQUESTS,), 2, PAGE_LIST_LENGTH * PAGE_TOKENS + 1), jax.random.fold_in(part_splits[5], 1), 2, PAGE_LIST_LENGTH * PAGE_TOKENS).astype(jnp.int32)
    out_weight = heavy_noise(keys[6], (QUERY_HEADS * HEAD_SIZE, D), (QUERY_HEADS * HEAD_SIZE) ** -0.5, 0.09375, ((0, 4),), (0, 1, 4, 2.0))
    return dict(queries=queries, newest_key_value=newest_key_value, kv_pages=kv_pages, fetch_slots=fetch_slots, block_table=block_table, prefix_len=prefix_len, out_weight=out_weight)


def reference(queries, newest_key_value, kv_pages, fetch_slots, block_table, prefix_len, out_weight):
    group_width = QUERY_HEADS // KEY_VALUE_HEADS
    group_of = (jnp.arange(TOTAL_REQUESTS) // REQ_GRP).astype(jnp.int32)
    page_owner = (block_table // GROUP_PAGE_LIMIT).astype(jnp.int32)
    column = (block_table % GROUP_PAGE_LIMIT).astype(jnp.int32)
    stored = fetch_slots[group_of[:, None], page_owner, column]
    page_index = (page_owner * PAGES_DEV + stored).astype(jnp.int32)
    score_scale = 1.0 / math.sqrt(HEAD_SIZE)

    def single(inputs):
        query_vector, newest_token, pages_used, length = inputs
        chosen_pages = kv_pages[pages_used]
        key_matrix = chosen_pages[:, 0].reshape(PAGE_LIST_LENGTH * PAGE_TOKENS, KEY_VALUE_HEADS, HEAD_SIZE).astype(jnp.float32)
        value_matrix = chosen_pages[:, 1].reshape(PAGE_LIST_LENGTH * PAGE_TOKENS, KEY_VALUE_HEADS, HEAD_SIZE).astype(jnp.float32)
        head_list = query_vector.reshape(KEY_VALUE_HEADS, group_width, HEAD_SIZE).astype(jnp.float32)
        newest_rows = newest_token.reshape(2, KEY_VALUE_HEADS, HEAD_SIZE).astype(jnp.float32)
        scores = jnp.einsum('kqd,pkd->kqp', head_list, key_matrix) * score_scale
        live_mask = jnp.arange(PAGE_LIST_LENGTH * PAGE_TOKENS) < length
        scores = jnp.where(live_mask[None, None, :], scores, -jnp.inf)
        own_score = jnp.einsum('kqd,kd->kq', head_list, newest_rows[0]) * score_scale
        row_top = jnp.maximum(lax.optimization_barrier(jnp.max(scores, axis=-1)), own_score)
        exp_terms = jnp.exp(scores - row_top[..., None])
        exp_own = jnp.exp(own_score - row_top)
        denom_sum = lax.optimization_barrier(jnp.sum(exp_terms, axis=-1)) + exp_own
        weights = (exp_terms / denom_sum[..., None]).astype(jnp.bfloat16).astype(jnp.float32)
        weight_own = (exp_own / denom_sum).astype(jnp.bfloat16).astype(jnp.float32)
        mixed = jnp.einsum('kqp,pkd->kqd', weights, value_matrix)
        mixed = mixed + weight_own[..., None] * newest_rows[1][:, None, :]
        return mixed.astype(jnp.bfloat16).reshape(QUERY_HEADS * HEAD_SIZE)
    mix = lax.map(single, (queries, newest_key_value, page_index, prefix_len))
    return jnp.dot(mix, out_weight, preferred_element_type=jnp.float32).astype(jnp.bfloat16)
```

```python
import functools
import math

import jax
import jax.numpy as jnp
from jax import lax
from jax.experimental import pallas as pl
from jax.experimental.pallas import tpu as pltpu
from jax.sharding import PartitionSpec as P

QUERY_HEADS = 64
KEY_VALUE_HEADS = 8
HEAD_SIZE = 128
GROUP_WIDTH = QUERY_HEADS // KEY_VALUE_HEADS
DEAD = -1e30
SCALE = math.log2(math.e) / math.sqrt(HEAD_SIZE)
MESH = pl.DeviceIdType.MESH
VMEM_LIMIT = 60 * 1024 * 1024
LANES = 128
RIGHT, LEFT = 0, 1

VMEM_SPEC = pl.BlockSpec(memory_space=pltpu.VMEM)
ANY_SPEC = pl.BlockSpec(memory_space=pl.ANY)


def routes():
    count, me = lax.axis_size("tp"), lax.axis_index("tp")
    pair, core, pairs = me // 2, me % 2, count // 2
    steps = [(i, b) for i in range(1, pairs) for b in range(2)] + [(0, 1)]
    return [(i, b, lax.rem(pair + i, pairs) * 2 + lax.rem(core + b, 2)) for i, b in steps]


def meet():
    barrier = pltpu.get_barrier_semaphore()
    groups, me = lax.axis_size("grp"), lax.axis_index("grp")
    ids = [{"tp": t} for _, _, t in routes()]
    ids += [{"grp": lax.rem(me + d, groups)} for d in range(1, groups)]
    for device in ids:
        pl.semaphore_signal(barrier, inc=1, device_id=device, device_id_type=MESH)
    pl.semaphore_wait(barrier, len(ids))


def remote(source, dest, send_sem, recv_sem, device):
    return pltpu.make_async_remote_copy(
        src_ref=source, dst_ref=dest, send_sem=send_sem, recv_sem=recv_sem,
        device_id=device, device_id_type=MESH,
    )


def turned(tile):
    a = tile.shape[0]
    if a < LANES:
        tile = jnp.concatenate([tile, jnp.zeros((LANES - a, LANES), jnp.float32)], axis=0)
    return tile.T


def weights_of(stats):
    top = functools.reduce(jnp.maximum, stats)
    parts = [jnp.exp2(s - top) for s in stats]
    total = functools.reduce(jnp.add, parts)
    inverse = 1.0 / total
    return [p * inverse for p in parts], top + jnp.log2(total)


def step_kernel(
    limit, q_in, kv_in, table_ref, length_ref, fetch_ref, new_ref, w_in, out_ref,
    q_ref, meta_ref, slots_ref, slots_smem, mask_ref, ksel_ref, vsel_ref,
    o_own, st_own, o_send, st_send, o_direct, st_direct, o_got, st_got, new_st,
    w_ref, mix_ref, acc_ref, core_send, core_got, far_send, far_got,
    small_send, small_recv, kv_send, kv_recv, q_send, q_recv, dir_send, dir_recv,
    chain_send, chain_recv, out_send, out_recv, own_sems, w_sems, *page_refs,
):
    kv_heads, groups, rows, cols = q_ref.shape
    owners, pages_dev, page, _ = page_refs[0].shape
    per_kv = cols // HEAD_SIZE
    heads = per_kv * kv_heads
    list_len = table_ref.shape[1]
    tokens = mask_ref.shape[2]
    pairs = owners // 2
    my_group, my_tp = lax.axis_index("grp"), lax.axis_index("tp")
    share = w_ref.shape[2]
    peers = routes()
    chained = kv_heads - 1

    lists = jnp.concatenate(
        [
            table_ref[...].astype(jnp.float32),
            jnp.zeros((rows, LANES - list_len), jnp.float32),
        ],
        axis=1,
    )
    meta_ref[my_group] = turned(lists)[: meta_ref.shape[1]]
    meta_ref[my_group, list_len : list_len + 1, :rows] = length_ref[...].astype(jnp.float32)
    slots_ref[my_tp] = jnp.zeros(slots_ref.shape[1:], jnp.int32)
    for g in range(groups):
        slots_ref[my_tp, g : g + 1, :limit] = fetch_ref[g]

    meet()

    small = []
    for i, (_, _, t) in enumerate(peers):
        small.append(
            remote(slots_ref.at[my_tp], slots_ref.at[my_tp], small_send.at[i], small_recv.at[i], {"tp": t})
        )
    for d in range(1, groups):
        i = owners - 2 + d
        small.append(
            remote(
                meta_ref.at[my_group], meta_ref.at[my_group], small_send.at[i], small_recv.at[i],
                {"grp": lax.rem(my_group + d, groups)},
            )
        )
    for copy in small:
        copy.start()

    def q_cols(k):
        return q_in.at[:, k * cols : (k + 1) * cols]

    def q_hop(k, way, d, source=None):
        group = my_group - (d - 1) if way == RIGHT else my_group + (d - 1)
        held = q_ref.at[k, group]
        nbr = my_group + 1 if way == RIGHT else my_group - 1
        return remote(
            held if source is None else source, held,
            q_send.at[k, way, d - 1], q_recv.at[k, way, d - 1], {"grp": nbr},
        )

    def can_send(way, d):
        if way == RIGHT:
            return (my_group + 1 < groups) & (my_group - (d - 1) >= 0)
        return (my_group >= 1) & (my_group + (d - 1) < groups)

    def can_get(way, d):
        return my_group - d >= 0 if way == RIGHT else my_group + d < groups

    def q_arrived(k, way, d):
        group = my_group - d if way == RIGHT else my_group + d
        held = q_ref.at[k, group]
        nbr = my_group - 1 if way == RIGHT else my_group + 1
        return remote(held, held, q_send.at[k, way, d - 1], q_recv.at[k, way, d - 1], {"grp": nbr})

    def own_q(k):
        return pltpu.make_async_copy(q_cols(k), q_ref.at[k, my_group], own_sems.at[k])

    def kv_copies(k, kind):
        n = 2 * k + kind

        def columns(t):
            first = (t * heads // GROUP_WIDTH + k) * HEAD_SIZE
            return kv_in.at[:, kind, :, pl.ds(pl.multiple_of(first, HEAD_SIZE), HEAD_SIZE)]

        dest = page_refs[n].at[my_tp]
        copies = [
            remote(columns(t), dest, kv_send.at[n, i], kv_recv.at[n, i], {"tp": t})
            for i, (_, _, t) in enumerate(peers)
        ]
        copies.append(pltpu.make_async_copy(columns(my_tp), dest, own_sems.at[kv_heads + n]))
        return copies

    kv_all = {}
    for k in range(kv_heads):
        for way in (RIGHT, LEFT):
            pl.when(can_send(way, 1))(lambda k=k, way=way: q_hop(k, way, 1, q_cols(k)).start())
        for kind in range(2):
            kv_all[k, kind] = kv_copies(k, kind)
            for copy in kv_all[k, kind]:
                copy.start()
        own_q(k).start()

    slot_ids = [(i, b, t) for i, b, t in peers] + [(0, 0, my_tp)]
    w_copies = []
    for s, (_, _, t) in enumerate(slot_ids):
        span = pl.ds(pl.multiple_of(t * share, 128), share)
        w_copies.append(pltpu.make_async_copy(w_in.at[:, span], w_ref.at[s], w_sems.at[s]))
        w_copies[-1].start()

    absent = jnp.full(st_got.shape[2:], DEAD, jnp.float32)
    nothing = jnp.zeros(o_got.shape[2:], jnp.bfloat16)

    @pl.when(my_group == 0)
    def _():
        o_got[RIGHT, my_group] = nothing
        st_got[RIGHT, my_group] = absent

    @pl.when(my_group == groups - 1)
    def _():
        o_got[LEFT, my_group] = nothing
        st_got[LEFT, my_group] = absent

    vsel_ref[:, HEAD_SIZE:] = jnp.ones((tokens, HEAD_SIZE), jnp.bfloat16)

    for copy in small:
        copy.wait()
    to_smem = pltpu.make_async_copy(slots_ref, slots_smem, own_sems.at[3 * kv_heads])
    to_smem.start()

    def relay(k, d):
        for way in (RIGHT, LEFT):

            @pl.when(can_get(way, d))
            def _():
                q_arrived(k, way, d).wait_recv()

            if d < groups - 1:
                pl.when(can_send(way, d + 1))(lambda: q_hop(k, way, d + 1).start())

    if groups > 2:
        relay(0, 1)

    lane_p = lax.broadcasted_iota(jnp.int32, (rows, page), 1)
    lane_j = lax.broadcasted_iota(jnp.int32, (rows, list_len), 1)

    def build(g, carry):
        both = turned(meta_ref[g])[:rows].astype(jnp.int32)
        entries = both[:, :list_len]
        length = both[:, list_len : list_len + 1]
        full, tail = length // page, length % page
        for n in range(owners * limit):
            same = entries == my_group * owners * limit + n
            whole = jnp.sum(jnp.where(same & (lane_j < full), 1.0, 0.0), axis=1, keepdims=True)
            part = jnp.sum(jnp.where(same & (lane_j == full), 1.0, 0.0), axis=1, keepdims=True)
            count = whole + jnp.where(lane_p < tail, part, 0.0)
            mask_ref[g, :, n * page : (n + 1) * page] = jnp.where(
                count > 0.0, jnp.log2(jnp.maximum(count, 1.0)), DEAD
            )
        return carry

    lax.fori_loop(0, groups, build, 0)

    for k in range(kv_heads):
        own_q(k).wait()
        new_key = new_ref[0, :, k * HEAD_SIZE : (k + 1) * HEAD_SIZE].astype(jnp.float32)
        lane = lax.broadcasted_iota(jnp.int32, (rows, LANES), 1)
        tile = jnp.zeros((rows, LANES), jnp.float32)
        for h in range(per_kv):
            q = q_ref[k, my_group, :, h * HEAD_SIZE : (h + 1) * HEAD_SIZE].astype(jnp.float32)
            tile = jnp.where(lane == h, jnp.sum(q * new_key, axis=1, keepdims=True) * SCALE, tile)
        new_st[k] = tile

    for d in range(1, groups - 1):
        for k in range(kv_heads):
            if (k, d) != (0, 1):
                relay(k, d)
    to_smem.wait()

    lane_s = lax.broadcasted_iota(jnp.int32, (rows, LANES), 1)
    unroll = 2 if per_kv % 2 == 0 else 1

    def attend(k, g):
        for n in range(owners * limit):
            t, c = n // limit, n % limit
            slot = jnp.maximum(slots_smem[t, g, c], 0)
            span = slice(n * page, (n + 1) * page)
            ksel_ref[span] = page_refs[2 * k][t, slot]
            vsel_ref[span, :HEAD_SIZE] = page_refs[2 * k + 1][t, slot]
        stats = jnp.zeros((rows, LANES), jnp.float32)
        for h0 in range(0, per_kv, unroll):
            q = jnp.concatenate(
                [
                    q_ref[k, g, :, h * HEAD_SIZE : (h + 1) * HEAD_SIZE]
                    for h in range(h0, h0 + unroll)
                ],
                axis=0,
            )
            s = lax.dot_general(
                q, ksel_ref[...], (((1,), (1,)), ((), ())), preferred_element_type=jnp.float32
            )
            s = s.reshape(unroll, rows, tokens) * SCALE + mask_ref[g][None]
            top = jnp.max(s, axis=2, keepdims=True)
            e = jnp.exp2(s - top).astype(jnp.bfloat16).reshape(unroll * rows, tokens)
            mixed = jnp.dot(e, vsel_ref[...], preferred_element_type=jnp.float32)
            total = mixed[:, HEAD_SIZE:]
            out = mixed[:, :HEAD_SIZE] / total
            span = slice(h0 * rows, (h0 + unroll) * rows)
            o_own[k, g, span] = out
            o_send[k, g, span] = out.astype(jnp.bfloat16)
            for u in range(unroll):
                level = top[u] + jnp.log2(total[u * rows : (u + 1) * rows])
                stats = jnp.where(lane_s == h0 + u, level, stats)
        st_own[k, g] = stats
        st_send[k, g] = turned(stats)[: st_send.shape[2]]

    def direct(k, g, d):
        return [
            remote(o_send.at[k, g], o_direct.at[k, d - 1], dir_send.at[k, d - 1, 0], dir_recv.at[k, d - 1, 0], {"grp": g}),
            remote(st_send.at[k, g], st_direct.at[k, d - 1], dir_send.at[k, d - 1, 1], dir_recv.at[k, d - 1, 1], {"grp": g}),
        ]

    def chain(way, g, nbr):
        return [
            remote(o_send.at[chained, g], o_got.at[way, g], chain_send.at[way, g, 0], chain_recv.at[way, g, 0], {"grp": nbr}),
            remote(st_send.at[chained, g], st_got.at[way, g], chain_send.at[way, g, 1], chain_recv.at[way, g, 1], {"grp": nbr}),
        ]

    def place(j):
        d = (j + 1) // 2
        left = lax.rem(j, 2) == 1
        g = jnp.where(left, my_group - d, my_group + d)
        return d, left, g, (g >= 0) & (g < groups)

    def attend_near(k):
        def body(j, carry):
            d, left, g, valid = place(j)

            @pl.when(valid)
            def _():
                @pl.when((d == groups - 1) & left)
                def _():
                    q_arrived(k, RIGHT, groups - 1).wait_recv()

                @pl.when((d == groups - 1) & jnp.logical_not(left))
                def _():
                    q_arrived(k, LEFT, groups - 1).wait_recv()

                attend(k, g)

                @pl.when(d > 0)
                def _():
                    for copy in direct(k, g, lax.rem(g - my_group + groups, groups)):
                        copy.start()

            return carry

        lax.fori_loop(0, 2 * groups - 1, body, 0)

    def attend_far(k):
        if groups > 1:
            for way in (RIGHT, LEFT):
                pl.when(can_get(way, groups - 1))(lambda way=way: q_arrived(k, way, groups - 1).wait_recv())

        def body(i, carry):
            d, left, g, valid = place(2 * groups - 2 - i)

            @pl.when(valid)
            def _():
                attend(k, g)

                @pl.when((my_group == 0) & (d > 0))
                def _():
                    for copy in chain(RIGHT, g, my_group + 1):
                        copy.start()

                @pl.when((my_group == groups - 1) & (d > 0))
                def _():
                    for copy in chain(LEFT, g, my_group - 1):
                        copy.start()

            return carry

        lax.fori_loop(0, 2 * groups - 1, body, 0)

    def spread_stats(tile):
        tile = jnp.concatenate(
            [tile, jnp.zeros((LANES - tile.shape[0], LANES), jnp.float32)], axis=0
        )
        return tile.T[:rows]

    def head_rows(h):
        return slice(h * rows, (h + 1) * rows)

    def pass_on():
        def body(i, carry):
            d, left, g, valid = place(2 * groups - 2 - i)
            between = (my_group > 0) & (my_group < groups - 1)

            def step(way, nbr, back):
                for copy in chain(way, g, back):
                    copy.wait_recv()
                (mine, other), level = weights_of([st_own[chained, g], spread_stats(st_got[way, g])])
                for h in range(per_kv):
                    out = mine[:, h : h + 1] * o_own[chained, g, head_rows(h)]
                    out += other[:, h : h + 1] * o_got[way, g, head_rows(h)].astype(jnp.float32)
                    o_send[chained, g, head_rows(h)] = out.astype(jnp.bfloat16)
                st_send[chained, g] = turned(level)[: st_send.shape[2]]
                for copy in chain(way, g, nbr):
                    copy.start()

            pl.when(valid & between & (d > 0) & jnp.logical_not(left))(
                lambda: step(RIGHT, my_group + 1, my_group - 1)
            )
            pl.when(valid & between & (d > 0) & left)(
                lambda: step(LEFT, my_group - 1, my_group + 1)
            )
            return carry

        lax.fori_loop(0, 2 * groups - 1, body, 0)

    def finish(k, others, levels):
        stats = [st_own[k, my_group], new_st[k]] + levels
        ways, _ = weights_of(stats)
        new_value = new_ref[1, :, k * HEAD_SIZE : (k + 1) * HEAD_SIZE].astype(jnp.float32)
        for h in range(per_kv):
            out = ways[0][:, h : h + 1] * o_own[k, my_group, head_rows(h)]
            out += ways[1][:, h : h + 1] * new_value
            for way, ref in zip(ways[2:], others):
                out += way[:, h : h + 1] * ref[head_rows(h)].astype(jnp.float32)
            mix_ref[k, :, h * HEAD_SIZE : (h + 1) * HEAD_SIZE] = out.astype(jnp.bfloat16)

    block = min(512, share)

    def project(k, s):
        def body(n, carry):
            span = pl.ds(pl.multiple_of(n * block, 128), block)
            made = jnp.dot(
                mix_ref[k], w_ref[s, k * cols : (k + 1) * cols, span],
                preferred_element_type=jnp.float32,
            )
            acc_ref[s, :, span] = made if k == 0 else acc_ref[s, :, span] + made
            return carry

        lax.fori_loop(0, share // block, body, 0)

    for k in range(kv_heads):
        for kind in range(2):
            for copy in kv_all[k, kind]:
                copy.wait()
        if k < chained:
            attend_near(k)
        else:
            attend_far(k)

    for k in range(chained):
        for d in range(1, groups):
            for copy in direct(k, lax.rem(my_group + d, groups), d):
                copy.wait()
        finish(
            k,
            [o_direct.at[k, d - 1] for d in range(1, groups)],
            [spread_stats(st_direct[k, d - 1]) for d in range(1, groups)],
        )
        if k == 0:
            for copy in w_copies:
                copy.wait()
        for s in range(owners):
            project(k, s)

    pass_on()

    for way in (RIGHT, LEFT):
        nbr = my_group - 1 if way == RIGHT else my_group + 1

        @pl.when(can_get(way, 1))
        def _():
            for copy in chain(way, my_group, nbr):
                copy.wait_recv()

    finish(
        chained,
        [o_got.at[way, my_group] for way in (RIGHT, LEFT)],
        [spread_stats(st_got[way, my_group]) for way in (RIGHT, LEFT)],
    )
    if chained == 0:
        for copy in w_copies:
            copy.wait()

    mate = {"tp": my_tp + 1 - 2 * lax.rem(my_tp, 2)}
    cores, fars = [None] * pairs, [None] * pairs
    index = {(i, b): s for s, (i, b, _) in enumerate(slot_ids)}
    for i in list(range(1, pairs)) + [0]:
        s = index[i, 1]
        project(chained, s)
        core_send[i] = acc_ref[s].astype(jnp.bfloat16)
        cores[i] = remote(core_send.at[i], core_got.at[i], out_send.at[0, i], out_recv.at[0, i], mate)
        cores[i].start()
        s = index[i, 0]
        project(chained, s)
        if i > 0:
            cores[i].wait()
            far_send[i - 1] = (acc_ref[s] + core_got[i].astype(jnp.float32)).astype(jnp.bfloat16)
            fars[i] = remote(
                far_send.at[i - 1], far_got.at[i - 1], out_send.at[1, i], out_recv.at[1, i],
                {"tp": slot_ids[s][2]},
            )
            fars[i].start()
    cores[0].wait()
    total = acc_ref[index[0, 0]] + core_got[0].astype(jnp.float32)
    for i in range(1, pairs):
        fars[i].wait()
        total = total + far_got[i - 1].astype(jnp.float32)
    out_ref[...] = total.astype(jnp.bfloat16)

    for k in range(kv_heads):
        for d in range(1, groups):
            for way in (RIGHT, LEFT):
                source = q_cols(k) if d == 1 else None
                pl.when(can_send(way, d))(lambda: q_hop(k, way, d, source).wait_send())
    for g in range(groups):
        for way in (RIGHT, LEFT):
            ahead = (my_group < g) if way == RIGHT else (my_group > g)
            nbr = my_group + 1 if way == RIGHT else my_group - 1

            @pl.when(ahead)
            def _():
                for copy in chain(way, g, nbr):
                    copy.wait_send()


def per_device(
    queries, newest_key_value, kv_pages, fetch_slots, block_table, prefix_len, out_weight
):
    T = lax.axis_size("tp")
    G = lax.axis_size("grp")
    tp_rank = lax.axis_index("tp")
    rows, cols = queries.shape
    heads = cols // HEAD_SIZE
    kv_dev = max(1, heads // GROUP_WIDTH)
    per_kv = heads // kv_dev
    width = kv_dev * HEAD_SIZE
    pages_dev, _, page, _ = kv_pages.shape
    list_len = block_table.shape[1]
    limit = fetch_slots.shape[2]
    model = out_weight.shape[1]
    dma = pltpu.SemaphoreType.DMA

    kv_first = (tp_rank * heads // GROUP_WIDTH) * HEAD_SIZE
    newest = lax.dynamic_slice_in_dim(newest_key_value, kv_first, width, 2).transpose(1, 0, 2)
    share = model // T
    pairs = T // 2
    bf16, f32, i32 = jnp.bfloat16, jnp.float32, jnp.int32
    vmem = pltpu.VMEM
    g_pad = -(-G // 8) * 8
    h_pad = -(-per_kv // 8) * 8
    m_pad = -(-(list_len + 1) // 8) * 8
    tokens = T * limit * page
    part = (per_kv * rows, HEAD_SIZE)
    near = max(1, kv_dev - 1)
    return pl.pallas_call(
        functools.partial(step_kernel, limit),
        out_shape=jax.ShapeDtypeStruct((rows, share), bf16),
        in_specs=[ANY_SPEC] * 2 + [VMEM_SPEC] * 4 + [ANY_SPEC],
        out_specs=VMEM_SPEC,
        scratch_shapes=[
            vmem((kv_dev, G, rows, per_kv * HEAD_SIZE), bf16),
            vmem((G, m_pad, LANES), f32),
            vmem((T, g_pad, LANES), i32),
            pltpu.SMEM((T, g_pad, LANES), i32),
            vmem((G, rows, tokens), f32),
            vmem((tokens, HEAD_SIZE), bf16),
            vmem((tokens, 2 * HEAD_SIZE), bf16),
            vmem((kv_dev, G, *part), f32),
            vmem((kv_dev, G, rows, LANES), f32),
            vmem((kv_dev, G, *part), bf16),
            vmem((kv_dev, G, h_pad, LANES), f32),
            vmem((near, G - 1, *part), bf16),
            vmem((near, G - 1, h_pad, LANES), f32),
            vmem((2, G, *part), bf16),
            vmem((2, G, h_pad, LANES), f32),
            vmem((kv_dev, rows, LANES), f32),
            vmem((T, out_weight.shape[0], share), bf16),
            vmem((kv_dev, rows, per_kv * HEAD_SIZE), bf16),
            vmem((T, rows, share), f32),
            vmem((pairs, rows, share), bf16),
            vmem((pairs, rows, share), bf16),
            vmem((max(1, pairs - 1), rows, share), bf16),
            vmem((max(1, pairs - 1), rows, share), bf16),
            dma((T + G - 2,)),
            dma((T + G - 2,)),
            dma((2 * kv_dev, T - 1)),
            dma((2 * kv_dev, T - 1)),
            dma((kv_dev, 2, G - 1)),
            dma((kv_dev, 2, G - 1)),
            dma((near, G - 1, 2)),
            dma((near, G - 1, 2)),
            dma((2, G, 2)),
            dma((2, G, 2)),
            dma((2, pairs)),
            dma((2, pairs)),
            dma((3 * kv_dev + 1,)),
            dma((T,)),
        ]
        + [vmem((T, pages_dev, page, HEAD_SIZE), bf16)] * (2 * kv_dev),
        compiler_params=pltpu.CompilerParams(
            collective_id=0, has_side_effects=True, vmem_limit_bytes=VMEM_LIMIT
        ),
        name="decode_step",
    )(
        queries, kv_pages, block_table, prefix_len.reshape(1, rows), fetch_slots, newest,
        out_weight,
    )


def solution(mesh):
    in_specs = (
        P(("rep", "grp"), "tp"),
        P(("rep", "grp"), None, None),
        P(("rep", "grp", "tp"), None, None, None),
        P("rep", ("grp", "tp"), None),
        P(("rep", "grp"), None),
        P(("rep", "grp")),
        P("tp", None),
    )
    out_specs = P(("rep", "grp"), "tp")
    return jax.shard_map(
        per_device, mesh=mesh, in_specs=in_specs, out_specs=out_specs, check_vma=False
    )
```

```python
import functools
import math

import jax
import jax.numpy as jnp
from jax import lax
from jax.experimental import pallas as pl
from jax.experimental.pallas import tpu as pltpu
from jax.sharding import PartitionSpec as P

QUERY_HEADS = 64
KEY_VALUE_HEADS = 8
HEAD_SIZE = 128
GROUP_WIDTH = QUERY_HEADS // KEY_VALUE_HEADS
DEAD = -1e30
SCALE = math.log2(math.e) / math.sqrt(HEAD_SIZE)
MESH = pl.DeviceIdType.MESH
VMEM_LIMIT = 60 * 1024 * 1024
LANES = 128
RIGHT, LEFT = 0, 1

VMEM_SPEC = pl.BlockSpec(memory_space=pltpu.VMEM)
ANY_SPEC = pl.BlockSpec(memory_space=pl.ANY)


def routes():
    count, me = lax.axis_size("tp"), lax.axis_index("tp")
    pair, core, pairs = me // 2, me % 2, count // 2
    steps = [(i, b) for i in range(1, pairs) for b in range(2)] + [(0, 1)]
    return [(i, b, lax.rem(pair + i, pairs) * 2 + lax.rem(core + b, 2)) for i, b in steps]


def meet():
    barrier = pltpu.get_barrier_semaphore()
    groups, me = lax.axis_size("grp"), lax.axis_index("grp")
    ids = [{"tp": t} for _, _, t in routes()]
    ids += [{"grp": lax.rem(me + d, groups)} for d in range(1, groups)]
    for device in ids:
        pl.semaphore_signal(barrier, inc=1, device_id=device, device_id_type=MESH)
    pl.semaphore_wait(barrier, len(ids))


def remote(source, dest, send_sem, recv_sem, device):
    return pltpu.make_async_remote_copy(
        src_ref=source, dst_ref=dest, send_sem=send_sem, recv_sem=recv_sem,
        device_id=device, device_id_type=MESH,
    )


def turned(tile):
    a = tile.shape[0]
    if a < LANES:
        tile = jnp.concatenate([tile, jnp.zeros((LANES - a, LANES), jnp.float32)], axis=0)
    return tile.T


def weights_of(stats):
    top = functools.reduce(jnp.maximum, stats)
    parts = [jnp.exp2(s - top) for s in stats]
    total = functools.reduce(jnp.add, parts)
    inverse = 1.0 / total
    return [p * inverse for p in parts], top + jnp.log2(total)


def step_kernel(
    limit, q_in, kv_in, table_in, length_in, fetch_in, new_in, w_in, out_ref,
    table_ref, length_ref, fetch_ref, pair_ref, new_ref, q_ref, meta_ref, slots_ref, slots_smem, mask_ref, ksel_ref, vsel_ref,
    o_own, st_own, o_send, st_send, o_direct, st_direct, o_got, st_got, new_st,
    w_ref, mix_ref, acc_ref, core_send, core_got, far_send, far_got,
    small_send, small_recv, kv_send, kv_recv, q_send, q_recv, dir_send, dir_recv,
    chain_send, chain_recv, out_send, out_recv, own_sems, w_sems, *page_refs,
):
    kv_heads, groups, rows, cols = q_ref.shape
    owners, pages_dev, page, _ = page_refs[0].shape
    per_kv = cols // HEAD_SIZE
    heads = per_kv * kv_heads
    list_len = table_ref.shape[0]
    tokens = mask_ref.shape[2]
    pairs = owners // 2
    my_group, my_tp = lax.axis_index("grp"), lax.axis_index("tp")
    share = w_ref.shape[2]
    peers = routes()
    chained = kv_heads - 1

    heads_done = 3 * kv_heads + 1
    first_kv = (my_tp * heads // GROUP_WIDTH) * HEAD_SIZE
    new_cols = pl.ds(pl.multiple_of(first_kv, HEAD_SIZE), kv_heads * HEAD_SIZE)
    loads = [
        pltpu.make_async_copy(source, dest, own_sems.at[heads_done + i])
        for i, (source, dest) in enumerate(
            [
                (table_in, table_ref),
                (length_in, length_ref),
                (fetch_in, fetch_ref),
                (new_in.at[:, :, new_cols], pair_ref),
            ]
        )
    ]
    for load in loads:
        load.start()

    meet()

    small = []
    for i, (_, _, t) in enumerate(peers):
        small.append(
            remote(slots_ref.at[my_tp], slots_ref.at[my_tp], small_send.at[i], small_recv.at[i], {"tp": t})
        )
    for d in range(1, groups):
        i = owners - 2 + d
        small.append(
            remote(
                meta_ref.at[my_group], meta_ref.at[my_group], small_send.at[i], small_recv.at[i],
                {"grp": lax.rem(my_group + d, groups)},
            )
        )
    def q_cols(k):
        return q_in.at[:, k * cols : (k + 1) * cols]

    def q_hop(k, way, d, source=None):
        group = my_group - (d - 1) if way == RIGHT else my_group + (d - 1)
        held = q_ref.at[k, group]
        nbr = my_group + 1 if way == RIGHT else my_group - 1
        return remote(
            held if source is None else source, held,
            q_send.at[k, way, d - 1], q_recv.at[k, way, d - 1], {"grp": nbr},
        )

    def can_send(way, d):
        if way == RIGHT:
            return (my_group + 1 < groups) & (my_group - (d - 1) >= 0)
        return (my_group >= 1) & (my_group + (d - 1) < groups)

    def can_get(way, d):
        return my_group - d >= 0 if way == RIGHT else my_group + d < groups

    def q_arrived(k, way, d):
        group = my_group - d if way == RIGHT else my_group + d
        held = q_ref.at[k, group]
        nbr = my_group - 1 if way == RIGHT else my_group + 1
        return remote(held, held, q_send.at[k, way, d - 1], q_recv.at[k, way, d - 1], {"grp": nbr})

    def own_q(k):
        return pltpu.make_async_copy(q_cols(k), q_ref.at[k, my_group], own_sems.at[k])

    def kv_columns(k, kind, t):
        first = (t * heads // GROUP_WIDTH + k) * HEAD_SIZE
        return kv_in.at[:, kind, :, pl.ds(pl.multiple_of(first, HEAD_SIZE), HEAD_SIZE)]

    def kv_copies(k, kind):
        n = 2 * k + kind
        dest = page_refs[n].at[my_tp]
        copies = [
            remote(kv_columns(k, kind, t), dest, kv_send.at[n, i], kv_recv.at[n, i], {"tp": t})
            for i, (_, _, t) in enumerate(peers)
        ]
        copies.append(
            pltpu.make_async_copy(kv_columns(k, kind, my_tp), dest, own_sems.at[kv_heads + n])
        )
        return copies

    def far_copy(k, kind, i, core):
        n = 2 * k + kind
        slot = 2 * (i - 1) + lax.rem(core + my_tp, 2)
        t = lax.rem(my_tp // 2 + i, pairs) * 2 + core
        return remote(
            kv_columns(k, kind, t), page_refs[n].at[my_tp], kv_send.at[n, slot], kv_recv.at[n, slot],
            {"tp": t},
        )

    def first_things():
        for load in loads:
            load.wait()
        meta_ref[my_group] = jnp.zeros(meta_ref.shape[1:], jnp.float32)
        meta_ref[my_group, :list_len, :rows] = table_ref[...].astype(jnp.float32)
        meta_ref[my_group, list_len : list_len + 1, :rows] = length_ref[...].astype(jnp.float32)
        slots_ref[my_tp] = jnp.zeros(slots_ref.shape[1:], jnp.int32)
        slots_ref[my_tp, :limit, :groups] = fetch_ref[...]
        for copy in small:
            copy.start()

    kv_all = {(k, kind): kv_copies(k, kind) for k in range(kv_heads) for kind in range(2)}
    for k in range(kv_heads):
        for way in (RIGHT, LEFT):
            pl.when(can_send(way, 1))(lambda k=k, way=way: q_hop(k, way, 1, q_cols(k)).start())
        for core in range(2):
            for kind in range(2):
                for i in range(1, pairs):
                    far_copy(k, kind, i, core).start()
            if k == 0 and core == 0:
                first_things()
        for kind in range(2):
            for copy in kv_all[k, kind][2 * (pairs - 1) :]:
                copy.start()
        own_q(k).start()

    slot_ids = [(i, b, t) for i, b, t in peers] + [(0, 0, my_tp)]
    w_copies = []
    for s, (_, _, t) in enumerate(slot_ids):
        span = pl.ds(pl.multiple_of(t * share, 128), share)
        w_copies.append(pltpu.make_async_copy(w_in.at[:, span], w_ref.at[s], w_sems.at[s]))
        w_copies[-1].start()

    absent = jnp.full(st_got.shape[2:], DEAD, jnp.float32)
    nothing = jnp.zeros(o_got.shape[2:], jnp.bfloat16)

    @pl.when(my_group == 0)
    def _():
        o_got[RIGHT, my_group] = nothing
        st_got[RIGHT, my_group] = absent

    @pl.when(my_group == groups - 1)
    def _():
        o_got[LEFT, my_group] = nothing
        st_got[LEFT, my_group] = absent

    vsel_ref[:, HEAD_SIZE:] = jnp.ones((tokens, HEAD_SIZE), jnp.bfloat16)

    for copy in small:
        copy.wait()
    to_smem = pltpu.make_async_copy(slots_ref, slots_smem, own_sems.at[3 * kv_heads])
    to_smem.start()

    def relay(k, d):
        for way in (RIGHT, LEFT):

            @pl.when(can_get(way, d))
            def _():
                q_arrived(k, way, d).wait_recv()

            if d < groups - 1:
                pl.when(can_send(way, d + 1))(lambda: q_hop(k, way, d + 1).start())

    if groups > 2:
        relay(0, 1)

    lane_p = lax.broadcasted_iota(jnp.int32, (rows, page), 1)
    lane_j = lax.broadcasted_iota(jnp.int32, (rows, list_len), 1)

    def build(g, carry):
        both = turned(meta_ref[g])[:rows].astype(jnp.int32)
        entries = both[:, :list_len]
        length = both[:, list_len : list_len + 1]
        full, tail = length // page, length % page
        for n in range(owners * limit):
            same = entries == my_group * owners * limit + n
            whole = jnp.sum(jnp.where(same & (lane_j < full), 1.0, 0.0), axis=1, keepdims=True)
            part = jnp.sum(jnp.where(same & (lane_j == full), 1.0, 0.0), axis=1, keepdims=True)
            count = whole + jnp.where(lane_p < tail, part, 0.0)
            mask_ref[g, :, n * page : (n + 1) * page] = jnp.where(
                count > 0.0, jnp.log2(jnp.maximum(count, 1.0)), DEAD
            )
        return carry

    lax.fori_loop(0, groups, build, 0)

    both = pair_ref[...].astype(jnp.float32)
    which = lax.broadcasted_iota(jnp.int32, both.shape, 1)
    for kind in range(2):
        new_ref[kind] = jnp.sum(jnp.where(which == kind, both, 0.0), axis=1)
    for k in range(kv_heads):
        own_q(k).wait()
        new_key = new_ref[0, :, k * HEAD_SIZE : (k + 1) * HEAD_SIZE]
        lane = lax.broadcasted_iota(jnp.int32, (rows, LANES), 1)
        tile = jnp.zeros((rows, LANES), jnp.float32)
        for h in range(per_kv):
            q = q_ref[k, my_group, :, h * HEAD_SIZE : (h + 1) * HEAD_SIZE].astype(jnp.float32)
            tile = jnp.where(lane == h, jnp.sum(q * new_key, axis=1, keepdims=True) * SCALE, tile)
        new_st[k] = tile

    for d in range(1, groups - 1):
        for k in range(kv_heads):
            if (k, d) != (0, 1):
                relay(k, d)
    to_smem.wait()

    lane_s = lax.broadcasted_iota(jnp.int32, (rows, LANES), 1)
    unroll = 2 if per_kv % 2 == 0 else 1

    def attend(k, g):
        for n in range(owners * limit):
            t, c = n // limit, n % limit
            slot = jnp.maximum(slots_smem[t, c, g], 0)
            span = slice(n * page, (n + 1) * page)
            ksel_ref[span] = page_refs[2 * k][t, slot]
            vsel_ref[span, :HEAD_SIZE] = page_refs[2 * k + 1][t, slot]
        stats = jnp.zeros((rows, LANES), jnp.float32)
        for h0 in range(0, per_kv, unroll):
            q = jnp.concatenate(
                [
                    q_ref[k, g, :, h * HEAD_SIZE : (h + 1) * HEAD_SIZE]
                    for h in range(h0, h0 + unroll)
                ],
                axis=0,
            )
            s = lax.dot_general(
                q, ksel_ref[...], (((1,), (1,)), ((), ())), preferred_element_type=jnp.float32
            )
            s = s.reshape(unroll, rows, tokens) * SCALE + mask_ref[g][None]
            top = jnp.max(s, axis=2, keepdims=True)
            e = jnp.exp2(s - top).astype(jnp.bfloat16).reshape(unroll * rows, tokens)
            mixed = jnp.dot(e, vsel_ref[...], preferred_element_type=jnp.float32)
            total = mixed[:, HEAD_SIZE:]
            out = mixed[:, :HEAD_SIZE] / total
            span = slice(h0 * rows, (h0 + unroll) * rows)
            o_own[k, g, span] = out
            o_send[k, g, span] = out.astype(jnp.bfloat16)
            for u in range(unroll):
                level = top[u] + jnp.log2(total[u * rows : (u + 1) * rows])
                stats = jnp.where(lane_s == h0 + u, level, stats)
        st_own[k, g] = stats
        st_send[k, g] = turned(stats)[: st_send.shape[2]]

    def direct(k, g, d):
        return [
            remote(o_send.at[k, g], o_direct.at[k, d - 1], dir_send.at[k, d - 1, 0], dir_recv.at[k, d - 1, 0], {"grp": g}),
            remote(st_send.at[k, g], st_direct.at[k, d - 1], dir_send.at[k, d - 1, 1], dir_recv.at[k, d - 1, 1], {"grp": g}),
        ]

    def chain(way, g, nbr):
        return [
            remote(o_send.at[chained, g], o_got.at[way, g], chain_send.at[way, g, 0], chain_recv.at[way, g, 0], {"grp": nbr}),
            remote(st_send.at[chained, g], st_got.at[way, g], chain_send.at[way, g, 1], chain_recv.at[way, g, 1], {"grp": nbr}),
        ]

    def place(j):
        d = (j + 1) // 2
        left = lax.rem(j, 2) == 1
        g = jnp.where(left, my_group - d, my_group + d)
        return d, left, g, (g >= 0) & (g < groups)

    def attend_near(k):
        def body(j, carry):
            d, left, g, valid = place(j)

            @pl.when(valid)
            def _():
                @pl.when((d == groups - 1) & left)
                def _():
                    q_arrived(k, RIGHT, groups - 1).wait_recv()

                @pl.when((d == groups - 1) & jnp.logical_not(left))
                def _():
                    q_arrived(k, LEFT, groups - 1).wait_recv()

                attend(k, g)

                @pl.when(d > 0)
                def _():
                    for copy in direct(k, g, lax.rem(g - my_group + groups, groups)):
                        copy.start()

            return carry

        lax.fori_loop(0, 2 * groups - 1, body, 0)

    def attend_far(k):
        if groups > 1:
            for way in (RIGHT, LEFT):
                pl.when(can_get(way, groups - 1))(lambda way=way: q_arrived(k, way, groups - 1).wait_recv())

        def body(i, carry):
            d, left, g, valid = place(2 * groups - 2 - i)

            @pl.when(valid)
            def _():
                attend(k, g)

                @pl.when((my_group == 0) & (d > 0))
                def _():
                    for copy in chain(RIGHT, g, my_group + 1):
                        copy.start()

                @pl.when((my_group == groups - 1) & (d > 0))
                def _():
                    for copy in chain(LEFT, g, my_group - 1):
                        copy.start()

            return carry

        lax.fori_loop(0, 2 * groups - 1, body, 0)

    def spread_stats(tile):
        tile = jnp.concatenate(
            [tile, jnp.zeros((LANES - tile.shape[0], LANES), jnp.float32)], axis=0
        )
        return tile.T[:rows]

    def head_rows(h):
        return slice(h * rows, (h + 1) * rows)

    def pass_on():
        def body(i, carry):
            d, left, g, valid = place(2 * groups - 2 - i)
            between = (my_group > 0) & (my_group < groups - 1)

            def step(way, nbr, back):
                for copy in chain(way, g, back):
                    copy.wait_recv()
                (mine, other), level = weights_of([st_own[chained, g], spread_stats(st_got[way, g])])
                for h in range(per_kv):
                    out = mine[:, h : h + 1] * o_own[chained, g, head_rows(h)]
                    out += other[:, h : h + 1] * o_got[way, g, head_rows(h)].astype(jnp.float32)
                    o_send[chained, g, head_rows(h)] = out.astype(jnp.bfloat16)
                st_send[chained, g] = turned(level)[: st_send.shape[2]]
                for copy in chain(way, g, nbr):
                    copy.start()

            pl.when(valid & between & (d > 0) & jnp.logical_not(left))(
                lambda: step(RIGHT, my_group + 1, my_group - 1)
            )
            pl.when(valid & between & (d > 0) & left)(
                lambda: step(LEFT, my_group - 1, my_group + 1)
            )
            return carry

        lax.fori_loop(0, 2 * groups - 1, body, 0)

    def finish(k, others, levels):
        stats = [st_own[k, my_group], new_st[k]] + levels
        ways, _ = weights_of(stats)
        new_value = new_ref[1, :, k * HEAD_SIZE : (k + 1) * HEAD_SIZE]
        for h in range(per_kv):
            out = ways[0][:, h : h + 1] * o_own[k, my_group, head_rows(h)]
            out += ways[1][:, h : h + 1] * new_value
            for way, ref in zip(ways[2:], others):
                out += way[:, h : h + 1] * ref[head_rows(h)].astype(jnp.float32)
            mix_ref[k, :, h * HEAD_SIZE : (h + 1) * HEAD_SIZE] = out.astype(jnp.bfloat16)

    block = min(512, share)

    def project(k, s):
        def body(n, carry):
            span = pl.ds(pl.multiple_of(n * block, 128), block)
            made = jnp.dot(
                mix_ref[k], w_ref[s, k * cols : (k + 1) * cols, span],
                preferred_element_type=jnp.float32,
            )
            acc_ref[s, :, span] = made if k == 0 else acc_ref[s, :, span] + made
            return carry

        lax.fori_loop(0, share // block, body, 0)

    for k in range(kv_heads):
        for kind in range(2):
            for copy in kv_all[k, kind]:
                copy.wait()
        if k < chained:
            attend_near(k)
        else:
            attend_far(k)

    for k in range(chained):
        for d in range(1, groups):
            for copy in direct(k, lax.rem(my_group + d, groups), d):
                copy.wait()
        finish(
            k,
            [o_direct.at[k, d - 1] for d in range(1, groups)],
            [spread_stats(st_direct[k, d - 1]) for d in range(1, groups)],
        )
        if k == 0:
            for copy in w_copies:
                copy.wait()
        for s in range(owners):
            project(k, s)

    pass_on()

    for way in (RIGHT, LEFT):
        nbr = my_group - 1 if way == RIGHT else my_group + 1

        @pl.when(can_get(way, 1))
        def _():
            for copy in chain(way, my_group, nbr):
                copy.wait_recv()

    finish(
        chained,
        [o_got.at[way, my_group] for way in (RIGHT, LEFT)],
        [spread_stats(st_got[way, my_group]) for way in (RIGHT, LEFT)],
    )
    if chained == 0:
        for copy in w_copies:
            copy.wait()

    mate = {"tp": my_tp + 1 - 2 * lax.rem(my_tp, 2)}
    cores, fars = [None] * pairs, [None] * pairs
    index = {(i, b): s for s, (i, b, _) in enumerate(slot_ids)}
    for i in list(range(1, pairs)) + [0]:
        s = index[i, 1]
        project(chained, s)
        core_send[i] = acc_ref[s].astype(jnp.bfloat16)
        cores[i] = remote(core_send.at[i], core_got.at[i], out_send.at[0, i], out_recv.at[0, i], mate)
        cores[i].start()
        s = index[i, 0]
        project(chained, s)
        if i > 0:
            cores[i].wait()
            far_send[i - 1] = (acc_ref[s] + core_got[i].astype(jnp.float32)).astype(jnp.bfloat16)
            fars[i] = remote(
                far_send.at[i - 1], far_got.at[i - 1], out_send.at[1, i], out_recv.at[1, i],
                {"tp": slot_ids[s][2]},
            )
            fars[i].start()
    cores[0].wait()
    total = acc_ref[index[0, 0]] + core_got[0].astype(jnp.float32)
    for i in range(1, pairs):
        fars[i].wait()
        total = total + far_got[i - 1].astype(jnp.float32)
    out_ref[...] = total.astype(jnp.bfloat16)

    for k in range(kv_heads):
        for d in range(1, groups):
            for way in (RIGHT, LEFT):
                source = q_cols(k) if d == 1 else None
                pl.when(can_send(way, d))(lambda: q_hop(k, way, d, source).wait_send())
    for g in range(groups):
        for way in (RIGHT, LEFT):
            ahead = (my_group < g) if way == RIGHT else (my_group > g)
            nbr = my_group + 1 if way == RIGHT else my_group - 1

            @pl.when(ahead)
            def _():
                for copy in chain(way, g, nbr):
                    copy.wait_send()


def per_device(
    queries, newest_key_value, kv_pages, fetch_slots, block_table, prefix_len, out_weight
):
    T = lax.axis_size("tp")
    G = lax.axis_size("grp")
    rows, cols = queries.shape
    heads = cols // HEAD_SIZE
    kv_dev = max(1, heads // GROUP_WIDTH)
    per_kv = heads // kv_dev
    width = kv_dev * HEAD_SIZE
    pages_dev, _, page, _ = kv_pages.shape
    list_len = block_table.shape[1]
    limit = fetch_slots.shape[2]
    model = out_weight.shape[1]
    dma = pltpu.SemaphoreType.DMA

    share = model // T
    pairs = T // 2
    bf16, f32, i32 = jnp.bfloat16, jnp.float32, jnp.int32
    vmem = pltpu.VMEM
    h_pad = -(-per_kv // 8) * 8
    m_pad = -(-(list_len + 1) // 8) * 8
    tokens = T * limit * page
    part = (per_kv * rows, HEAD_SIZE)
    near = max(1, kv_dev - 1)
    return pl.pallas_call(
        functools.partial(step_kernel, limit),
        out_shape=jax.ShapeDtypeStruct((rows, share), bf16),
        in_specs=[ANY_SPEC] * 7,
        out_specs=VMEM_SPEC,
        scratch_shapes=[
            vmem((list_len, rows), i32),
            vmem((1, rows), i32),
            vmem((limit, G), i32),
            vmem((rows, 2, width), bf16),
            vmem((2, rows, width), f32),
            vmem((kv_dev, G, rows, per_kv * HEAD_SIZE), bf16),
            vmem((G, m_pad, LANES), f32),
            vmem((T, 8, LANES), i32),
            pltpu.SMEM((T, 8, LANES), i32),
            vmem((G, rows, tokens), f32),
            vmem((tokens, HEAD_SIZE), bf16),
            vmem((tokens, 2 * HEAD_SIZE), bf16),
            vmem((kv_dev, G, *part), f32),
            vmem((kv_dev, G, rows, LANES), f32),
            vmem((kv_dev, G, *part), bf16),
            vmem((kv_dev, G, h_pad, LANES), f32),
            vmem((near, G - 1, *part), bf16),
            vmem((near, G - 1, h_pad, LANES), f32),
            vmem((2, G, *part), bf16),
            vmem((2, G, h_pad, LANES), f32),
            vmem((kv_dev, rows, LANES), f32),
            vmem((T, out_weight.shape[0], share), bf16),
            vmem((kv_dev, rows, per_kv * HEAD_SIZE), bf16),
            vmem((T, rows, share), f32),
            vmem((pairs, rows, share), bf16),
            vmem((pairs, rows, share), bf16),
            vmem((max(1, pairs - 1), rows, share), bf16),
            vmem((max(1, pairs - 1), rows, share), bf16),
            dma((T + G - 2,)),
            dma((T + G - 2,)),
            dma((2 * kv_dev, T - 1)),
            dma((2 * kv_dev, T - 1)),
            dma((kv_dev, 2, G - 1)),
            dma((kv_dev, 2, G - 1)),
            dma((near, G - 1, 2)),
            dma((near, G - 1, 2)),
            dma((2, G, 2)),
            dma((2, G, 2)),
            dma((2, pairs)),
            dma((2, pairs)),
            dma((3 * kv_dev + 5,)),
            dma((T,)),
        ]
        + [vmem((T, pages_dev, page, HEAD_SIZE), bf16)] * (2 * kv_dev),
        compiler_params=pltpu.CompilerParams(
            collective_id=0, has_side_effects=True, vmem_limit_bytes=VMEM_LIMIT
        ),
        name="decode_step",
    )(
        queries, kv_pages, block_table.T, prefix_len.reshape(1, rows),
        fetch_slots.reshape(G, limit).T, newest_key_value, out_weight,
    )


def solution(mesh):
    in_specs = (
        P(("rep", "grp"), "tp"),
        P(("rep", "grp"), None, None),
        P(("rep", "grp", "tp"), None, None, None),
        P("rep", ("grp", "tp"), None),
        P(("rep", "grp"), None),
        P(("rep", "grp")),
        P("tp", None),
    )
    out_specs = P(("rep", "grp"), "tp")
    return jax.shard_map(
        per_device, mesh=mesh, in_specs=in_specs, out_specs=out_specs, check_vma=False
    )
```

```python
import functools
import math

import jax
import jax.numpy as jnp
from jax import lax
from jax.experimental import pallas as pl
from jax.experimental.pallas import tpu as pltpu
from jax.sharding import PartitionSpec as P

QUERY_HEADS = 64
KEY_VALUE_HEADS = 8
HEAD_SIZE = 128
GROUP_WIDTH = QUERY_HEADS // KEY_VALUE_HEADS
DEAD = -1e30
SCALE = math.log2(math.e) / math.sqrt(HEAD_SIZE)
MESH = pl.DeviceIdType.MESH
VMEM_LIMIT = 60 * 1024 * 1024
LANES = 128
RIGHT, LEFT = 0, 1

VMEM_SPEC = pl.BlockSpec(memory_space=pltpu.VMEM)
ANY_SPEC = pl.BlockSpec(memory_space=pl.ANY)


def routes():
    count, me = lax.axis_size("tp"), lax.axis_index("tp")
    pair, core, pairs = me // 2, me % 2, count // 2
    steps = [(i, b) for i in range(1, pairs) for b in range(2)] + [(0, 1)]
    return [(i, b, lax.rem(pair + i, pairs) * 2 + lax.rem(core + b, 2)) for i, b in steps]


def meet():
    barrier = pltpu.get_barrier_semaphore()
    groups, me = lax.axis_size("grp"), lax.axis_index("grp")
    ids = [{"tp": t} for _, _, t in routes()]
    ids += [{"grp": lax.rem(me + d, groups)} for d in range(1, groups)]
    for device in ids:
        pl.semaphore_signal(barrier, inc=1, device_id=device, device_id_type=MESH)
    pl.semaphore_wait(barrier, len(ids))


def remote(source, dest, send_sem, recv_sem, device):
    return pltpu.make_async_remote_copy(
        src_ref=source, dst_ref=dest, send_sem=send_sem, recv_sem=recv_sem,
        device_id=device, device_id_type=MESH,
    )


def turned(tile):
    a = tile.shape[0]
    if a < LANES:
        tile = jnp.concatenate([tile, jnp.zeros((LANES - a, LANES), jnp.float32)], axis=0)
    return tile.T


def weights_of(stats):
    top = functools.reduce(jnp.maximum, stats)
    parts = [jnp.exp2(s - top) for s in stats]
    total = functools.reduce(jnp.add, parts)
    inverse = 1.0 / total
    return [p * inverse for p in parts], top + jnp.log2(total)


def step_kernel(
    limit, q_in, kv_in, table_in, length_in, fetch_in, new_in, w_in, out_ref,
    table_ref, length_ref, fetch_ref, pair_ref, new_ref, q_ref, meta_ref, slots_ref, slots_smem, mask_ref, ksel_ref, vsel_ref,
    o_own, st_own, o_send, st_send, o_mid, st_mid, o_got, st_got, new_st,
    w_ref, mix_ref, acc_ref, core_send, core_got, far_send, far_got,
    small_send, small_recv, kv_send, kv_recv, q_send, q_recv, part_send, mid_recv, got_recv, out_send, out_recv, own_sems, w_sems, *page_refs,
):
    kv_heads, groups, rows, cols = q_ref.shape
    owners, pages_dev, page, _ = page_refs[0].shape
    per_kv = cols // HEAD_SIZE
    heads = per_kv * kv_heads
    list_len = table_ref.shape[0]
    tokens = mask_ref.shape[2]
    pairs = owners // 2
    my_group, my_tp = lax.axis_index("grp"), lax.axis_index("tp")
    share = w_ref.shape[2]
    peers = routes()
    chained = kv_heads - 1

    heads_done = 3 * kv_heads + 1
    first_kv = (my_tp * heads // GROUP_WIDTH) * HEAD_SIZE
    new_cols = pl.ds(pl.multiple_of(first_kv, HEAD_SIZE), kv_heads * HEAD_SIZE)
    loads = [
        pltpu.make_async_copy(source, dest, own_sems.at[heads_done + i])
        for i, (source, dest) in enumerate(
            [
                (table_in, table_ref),
                (length_in, length_ref),
                (fetch_in, fetch_ref),
                (new_in.at[:, :, new_cols], pair_ref),
            ]
        )
    ]
    for load in loads:
        load.start()

    meet()

    small = []
    for i, (_, _, t) in enumerate(peers):
        small.append(
            remote(slots_ref.at[my_tp], slots_ref.at[my_tp], small_send.at[i], small_recv.at[i], {"tp": t})
        )
    for d in range(1, groups):
        i = owners - 2 + d
        small.append(
            remote(
                meta_ref.at[my_group], meta_ref.at[my_group], small_send.at[i], small_recv.at[i],
                {"grp": lax.rem(my_group + d, groups)},
            )
        )
    def q_cols(k):
        return q_in.at[:, k * cols : (k + 1) * cols]

    def q_hop(k, way, d, source=None):
        group = my_group - (d - 1) if way == RIGHT else my_group + (d - 1)
        held = q_ref.at[k, group]
        nbr = my_group + 1 if way == RIGHT else my_group - 1
        return remote(
            held if source is None else source, held,
            q_send.at[k, way, d - 1], q_recv.at[k, way, d - 1], {"grp": nbr},
        )

    def can_send(way, d):
        if way == RIGHT:
            return (my_group + 1 < groups) & (my_group - (d - 1) >= 0)
        return (my_group >= 1) & (my_group + (d - 1) < groups)

    def can_get(way, d):
        return my_group - d >= 0 if way == RIGHT else my_group + d < groups

    def q_arrived(k, way, d):
        group = my_group - d if way == RIGHT else my_group + d
        held = q_ref.at[k, group]
        nbr = my_group - 1 if way == RIGHT else my_group + 1
        return remote(held, held, q_send.at[k, way, d - 1], q_recv.at[k, way, d - 1], {"grp": nbr})

    def own_q(k):
        return pltpu.make_async_copy(q_cols(k), q_ref.at[k, my_group], own_sems.at[k])

    def kv_columns(k, kind, t):
        first = (t * heads // GROUP_WIDTH + k) * HEAD_SIZE
        return kv_in.at[:, kind, :, pl.ds(pl.multiple_of(first, HEAD_SIZE), HEAD_SIZE)]

    def kv_copies(k, kind):
        n = 2 * k + kind
        dest = page_refs[n].at[my_tp]
        copies = [
            remote(kv_columns(k, kind, t), dest, kv_send.at[n, i], kv_recv.at[n, i], {"tp": t})
            for i, (_, _, t) in enumerate(peers)
        ]
        copies.append(
            pltpu.make_async_copy(kv_columns(k, kind, my_tp), dest, own_sems.at[kv_heads + n])
        )
        return copies

    def far_copy(k, kind, i, core):
        n = 2 * k + kind
        slot = 2 * (i - 1) + lax.rem(core + my_tp, 2)
        t = lax.rem(my_tp // 2 + i, pairs) * 2 + core
        return remote(
            kv_columns(k, kind, t), page_refs[n].at[my_tp], kv_send.at[n, slot], kv_recv.at[n, slot],
            {"tp": t},
        )

    def first_things():
        for load in loads:
            load.wait()
        meta_ref[my_group] = jnp.zeros(meta_ref.shape[1:], jnp.float32)
        meta_ref[my_group, :list_len, :rows] = table_ref[...].astype(jnp.float32)
        meta_ref[my_group, list_len : list_len + 1, :rows] = length_ref[...].astype(jnp.float32)
        slots_ref[my_tp] = jnp.zeros(slots_ref.shape[1:], jnp.int32)
        slots_ref[my_tp, :limit, :groups] = fetch_ref[...]
        for copy in small:
            copy.start()

    kv_all = {(k, kind): kv_copies(k, kind) for k in range(kv_heads) for kind in range(2)}
    for k in range(kv_heads):
        for way in (RIGHT, LEFT):
            pl.when(can_send(way, 1))(lambda k=k, way=way: q_hop(k, way, 1, q_cols(k)).start())
        for core in range(2):
            for kind in range(2):
                for i in range(1, pairs):
                    far_copy(k, kind, i, core).start()
            if k == 0 and core == 0:
                first_things()
        for kind in range(2):
            for copy in kv_all[k, kind][2 * (pairs - 1) :]:
                copy.start()
        own_q(k).start()

    slot_ids = [(i, b, t) for i, b, t in peers] + [(0, 0, my_tp)]
    w_copies = []
    for s, (_, _, t) in enumerate(slot_ids):
        span = pl.ds(pl.multiple_of(t * share, 128), share)
        w_copies.append(pltpu.make_async_copy(w_in.at[:, span], w_ref.at[s], w_sems.at[s]))
        w_copies[-1].start()

    vsel_ref[:, HEAD_SIZE:] = jnp.ones((tokens, HEAD_SIZE), jnp.bfloat16)

    for copy in small:
        copy.wait_recv()
    to_smem = pltpu.make_async_copy(slots_ref, slots_smem, own_sems.at[3 * kv_heads])
    to_smem.start()

    def relay(k, d):
        for way in (RIGHT, LEFT):

            @pl.when(can_get(way, d))
            def _():
                q_arrived(k, way, d).wait_recv()

            if d < groups - 1:
                pl.when(can_send(way, d + 1))(lambda: q_hop(k, way, d + 1).start())

    lane_p = lax.broadcasted_iota(jnp.int32, (rows, page), 1)
    lane_j = lax.broadcasted_iota(jnp.int32, (rows, list_len), 1)

    def build(g, carry):
        both = turned(meta_ref[g])[:rows].astype(jnp.int32)
        entries = both[:, :list_len]
        length = both[:, list_len : list_len + 1]
        full, tail = length // page, length % page
        for n in range(owners * limit):
            same = entries == my_group * owners * limit + n
            whole = jnp.sum(jnp.where(same & (lane_j < full), 1.0, 0.0), axis=1, keepdims=True)
            part = jnp.sum(jnp.where(same & (lane_j == full), 1.0, 0.0), axis=1, keepdims=True)
            count = whole + jnp.where(lane_p < tail, part, 0.0)
            mask_ref[g, :, n * page : (n + 1) * page] = jnp.where(
                count > 0.0, jnp.log2(jnp.maximum(count, 1.0)), DEAD
            )
        return carry


    lane_s = lax.broadcasted_iota(jnp.int32, (rows, LANES), 1)
    unroll = 2 if per_kv % 2 == 0 else 1

    def attend(k, g):
        for n in range(owners * limit):
            t, c = n // limit, n % limit
            slot = jnp.maximum(slots_smem[t, c, g], 0)
            span = slice(n * page, (n + 1) * page)
            ksel_ref[span] = page_refs[2 * k][t, slot]
            vsel_ref[span, :HEAD_SIZE] = page_refs[2 * k + 1][t, slot]
        stats = jnp.zeros((rows, LANES), jnp.float32)
        for h0 in range(0, per_kv, unroll):
            q = jnp.concatenate(
                [
                    q_ref[k, g, :, h * HEAD_SIZE : (h + 1) * HEAD_SIZE]
                    for h in range(h0, h0 + unroll)
                ],
                axis=0,
            )
            s = lax.dot_general(
                q, ksel_ref[...], (((1,), (1,)), ((), ())), preferred_element_type=jnp.float32
            )
            s = s.reshape(unroll, rows, tokens) * SCALE + mask_ref[g][None]
            top = jnp.max(s, axis=2, keepdims=True)
            e = jnp.exp2(s - top).astype(jnp.bfloat16).reshape(unroll * rows, tokens)
            mixed = jnp.dot(e, vsel_ref[...], preferred_element_type=jnp.float32)
            total = mixed[:, HEAD_SIZE:]
            out = mixed[:, :HEAD_SIZE] / total
            span = slice(h0 * rows, (h0 + unroll) * rows)
            o_own[k, g, span] = out
            o_send[k, g, span] = out.astype(jnp.bfloat16)
            for u in range(unroll):
                level = top[u] + jnp.log2(total[u * rows : (u + 1) * rows])
                stats = jnp.where(lane_s == h0 + u, level, stats)
        st_own[k, g] = stats
        st_send[k, g] = turned(stats)[: st_send.shape[2]]

    pair = my_group // 2
    neighbour = my_group + 1 - 2 * lax.rem(my_group, 2)

    def carried(g):
        return (g // 2 != pair) & ((g > my_group) == (lax.rem(my_group, 2) == 1))

    def to_mid(k, g):
        return [
            remote(o_send.at[k, g], o_mid.at[k, g], part_send.at[k, g, 0], mid_recv.at[k, g, 0], {"grp": neighbour}),
            remote(st_send.at[k, g], st_mid.at[k, g], part_send.at[k, g, 1], mid_recv.at[k, g, 1], {"grp": neighbour}),
        ]

    def to_end(k, g, group):
        return [
            remote(o_send.at[k, g], o_got.at[k, pair], part_send.at[k, g, 0], got_recv.at[k, pair, 0], {"grp": group}),
            remote(st_send.at[k, g], st_got.at[k, pair], part_send.at[k, g, 1], got_recv.at[k, pair, 1], {"grp": group}),
        ]

    def from_pair(k, n):
        return [
            remote(o_got.at[k, n], o_got.at[k, n], part_send.at[k, 0, 0], got_recv.at[k, n, 0], {"grp": neighbour}),
            remote(st_got.at[k, n], st_got.at[k, n], part_send.at[k, 0, 1], got_recv.at[k, n, 1], {"grp": neighbour}),
        ]

    def place(j):
        d = (j + 1) // 2
        left = lax.rem(j, 2) == 1
        g = jnp.where(left, my_group - d, my_group + d)
        return d, left, g, (g >= 0) & (g < groups)

    def attend_some(k, first, last, far=False):
        low, high = max(0, 2 * first - 1), 2 * last + 1

        def body(i, carry):
            d, left, g, valid = place(low + high - 1 - i if far else i)

            @pl.when(valid)
            def _():
                if groups > 1:

                    @pl.when((d == groups - 1) & left)
                    def _():
                        q_arrived(k, RIGHT, groups - 1).wait_recv()

                    @pl.when((d == groups - 1) & jnp.logical_not(left))
                    def _():
                        q_arrived(k, LEFT, groups - 1).wait_recv()

                attend(k, g)

                @pl.when(g == neighbour)
                def _():
                    for copy in to_end(k, g, neighbour):
                        copy.start()

                @pl.when((g // 2 != pair) & jnp.logical_not(carried(g)))
                def _():
                    for copy in to_mid(k, g):
                        copy.start()

            return carry

        lax.fori_loop(low, high, body, 0)

    def spread_stats(tile):
        tile = jnp.concatenate(
            [tile, jnp.zeros((LANES - tile.shape[0], LANES), jnp.float32)], axis=0
        )
        return tile.T[:rows]

    def head_rows(h):
        return slice(h * rows, (h + 1) * rows)

    def pass_on(k, before, after, far=True):
        def body(i, carry):
            _, _, g, valid = place(2 * groups - 2 - i if far else i + 1)
            before(i)

            @pl.when(valid & carried(g))
            def _():
                for copy in to_mid(k, g):
                    copy.wait_recv()
                (mine, other), level = weights_of([st_own[k, g], spread_stats(st_mid[k, g])])
                for h in range(per_kv):
                    out = mine[:, h : h + 1] * o_own[k, g, head_rows(h)]
                    out += other[:, h : h + 1] * o_mid[k, g, head_rows(h)].astype(jnp.float32)
                    o_send[k, g, head_rows(h)] = out.astype(jnp.bfloat16)
                st_send[k, g] = turned(level)[: st_send.shape[2]]
                for copy in to_end(k, g, g):
                    copy.start()

            after(i)
            return carry

        lax.fori_loop(0, 2 * groups - 2, body, 0)

    def finish(k):
        others = [o_got.at[k, n] for n in range(groups // 2)]
        for n in range(groups // 2):
            for copy in from_pair(k, n):
                copy.wait_recv()
        levels = [spread_stats(st_got[k, n]) for n in range(groups // 2)]
        stats = [st_own[k, my_group], new_st[k]] + levels
        ways, _ = weights_of(stats)
        new_value = new_ref[1, :, k * HEAD_SIZE : (k + 1) * HEAD_SIZE]
        for h in range(per_kv):
            out = ways[0][:, h : h + 1] * o_own[k, my_group, head_rows(h)]
            out += ways[1][:, h : h + 1] * new_value
            for way, ref in zip(ways[2:], others):
                out += way[:, h : h + 1] * ref[head_rows(h)].astype(jnp.float32)
            mix_ref[k, :, h * HEAD_SIZE : (h + 1) * HEAD_SIZE] = out.astype(jnp.bfloat16)

    halves = 2 if share % 256 == 0 else 1
    half = share // halves
    block = half

    def project(k, s, part):
        def body(n, carry):
            span = pl.ds(pl.multiple_of(part * half + n * block, 128), block)
            made = jnp.dot(
                mix_ref[k], w_ref[s, k * cols : (k + 1) * cols, span],
                preferred_element_type=jnp.float32,
            )
            acc_ref[s, :, span] = made if k == 0 else acc_ref[s, :, span] + made
            return carry

        lax.fori_loop(0, half // block, body, 0)

    def nothing(i):
        pass

    def new_token():
        both = pair_ref[...].astype(jnp.float32)
        which = lax.broadcasted_iota(jnp.int32, both.shape, 1)
        for kind in range(2):
            new_ref[kind] = jnp.sum(jnp.where(which == kind, both, 0.0), axis=1)
        for k in range(kv_heads):
            own_q(k).wait()
            new_key = new_ref[0, :, k * HEAD_SIZE : (k + 1) * HEAD_SIZE]
            lane = lax.broadcasted_iota(jnp.int32, (rows, LANES), 1)
            tile = jnp.zeros((rows, LANES), jnp.float32)
            for h in range(per_kv):
                q = q_ref[k, my_group, :, h * HEAD_SIZE : (h + 1) * HEAD_SIZE].astype(jnp.float32)
                tile = jnp.where(lane == h, jnp.sum(q * new_key, axis=1, keepdims=True) * SCALE, tile)
            new_st[k] = tile

    def kv_arrived(k):
        for kind in range(2):
            for copy in kv_all[k, kind][:-1]:
                copy.wait_recv()
            kv_all[k, kind][-1].wait()

    steps = 2 * groups - 2
    early = min(owners, max(0, steps - 4))
    late = min(owners - early, max(0, steps - early - 2))

    def whole(k, s):
        for part in range(halves):
            project(k, s, part)

    core = lax.rem(my_tp, 2)

    def hop(d, heads_of):
        if d < groups - 1:
            for k in heads_of:
                relay(k, d)

    hop(1, [0])
    lax.fori_loop(0, groups // 2, build, 0)
    hop(1, range(1, kv_heads))
    lax.fori_loop(groups // 2, groups, build, 0)
    to_smem.wait()
    new_token()

    reach = min(1, groups - 1)

    @pl.when(core == 0)
    def _():
        kv_arrived(0)
        attend_some(0, 0, reach)

    hop(2, [0])

    @pl.when(core == 1)
    def _():
        kv_arrived(0)
        attend_some(0, 0, reach)

    hop(2, range(1, kv_heads))
    for d in range(2, groups):
        if d > 2:
            hop(d, range(kv_heads))
        attend_some(0, d, d)

    def ahead(k):
        pass_on(k, nothing, nothing, far=False)

    def catch_up(k):
        kv_arrived(k)
        attend_some(k, 0, groups - 1, far=True)

    for k in range(1, kv_heads):

        @pl.when(core == 0)
        def _():
            catch_up(k)
            ahead(k - 1)

        @pl.when(core == 1)
        def _():
            ahead(k - 1)
            catch_up(k)

    for copy in w_copies:
        copy.wait()

    @pl.when(core == 0)
    def _():
        pass_on(chained, nothing, nothing)
        for k in range(chained):
            finish(k)
            for s in range(owners):
                whole(k, s)

    @pl.when(core == 1)
    def _():
        for k in range(chained):
            finish(k)
            if k < chained - 1:
                for s in range(owners):
                    whole(k, s)
        if chained == 0:
            pass_on(chained, nothing, nothing)
        else:
            pass_on(
                chained,
                lambda i: pl.when(i < early)(lambda: whole(chained - 1, i)),
                lambda i: pl.when((i > early) & (i <= early + late))(
                    lambda: whole(chained - 1, i - 1)
                ),
            )
            for s in range(early + late, owners):
                whole(chained - 1, s)

    finish(chained)

    mate = {"tp": my_tp + 1 - 2 * lax.rem(my_tp, 2)}
    cores, fars = {}, {}

    def last(s, span):
        made = jnp.dot(
            mix_ref[chained], w_ref[s, chained * cols : (chained + 1) * cols, span],
            preferred_element_type=jnp.float32,
        )
        return made if chained == 0 else acc_ref[s, :, span] + made

    index = {(i, b): s for s, (i, b, _) in enumerate(slot_ids)}
    spans = [slice(p * half, (p + 1) * half) for p in range(halves)]
    for i in list(range(1, pairs)) + [0]:
        for p, span in enumerate(spans):
            s = index[i, 1]
            core_send[i, :, span] = last(s, span).astype(jnp.bfloat16)
            cores[i, p] = remote(
                core_send.at[i, :, span], core_got.at[i, :, span],
                out_send.at[0, i, p], out_recv.at[0, i, p], mate,
            )
            cores[i, p].start()
        for p, span in enumerate(spans):
            s = index[i, 0]
            made = last(s, span)
            if i == 0:
                acc_ref[s, :, span] = made
            else:
                cores[i, p].wait_recv()
                far_send[i - 1, :, span] = (
                    made + core_got[i, :, span].astype(jnp.float32)
                ).astype(jnp.bfloat16)
                fars[i, p] = remote(
                    far_send.at[i - 1, :, span], far_got.at[i - 1, :, span],
                    out_send.at[1, i, p], out_recv.at[1, i, p], {"tp": slot_ids[s][2]},
                )
                fars[i, p].start()
    for p, span in enumerate(spans):
        cores[0, p].wait_recv()
        total = acc_ref[index[0, 0], :, span] + core_got[0, :, span].astype(jnp.float32)
        for i in range(1, pairs):
            fars[i, p].wait_recv()
            total = total + far_got[i - 1, :, span].astype(jnp.float32)
        out_ref[:, span] = total.astype(jnp.bfloat16)

    sent = small + list(cores.values()) + list(fars.values())
    for copies in kv_all.values():
        sent += copies[:-1]
    for copy in sent:
        copy.wait_send()
    for k in range(kv_heads):
        for d in range(1, groups):
            for way in (RIGHT, LEFT):
                source = q_cols(k) if d == 1 else None
                pl.when(can_send(way, d))(lambda: q_hop(k, way, d, source).wait_send())
    for k in range(kv_heads):
        for g in range(groups):

            @pl.when(my_group != g)
            def _():
                for copy in to_mid(k, g):
                    copy.wait_send()


def per_device(
    queries, newest_key_value, kv_pages, fetch_slots, block_table, prefix_len, out_weight
):
    T = lax.axis_size("tp")
    G = lax.axis_size("grp")
    rows, cols = queries.shape
    heads = cols // HEAD_SIZE
    kv_dev = max(1, heads // GROUP_WIDTH)
    per_kv = heads // kv_dev
    width = kv_dev * HEAD_SIZE
    pages_dev, _, page, _ = kv_pages.shape
    list_len = block_table.shape[1]
    limit = fetch_slots.shape[2]
    model = out_weight.shape[1]
    dma = pltpu.SemaphoreType.DMA

    share = model // T
    pairs = T // 2
    bf16, f32, i32 = jnp.bfloat16, jnp.float32, jnp.int32
    vmem = pltpu.VMEM
    h_pad = -(-per_kv // 8) * 8
    m_pad = -(-(list_len + 1) // 8) * 8
    tokens = T * limit * page
    part = (per_kv * rows, HEAD_SIZE)
    return pl.pallas_call(
        functools.partial(step_kernel, limit),
        out_shape=jax.ShapeDtypeStruct((rows, share), bf16),
        in_specs=[ANY_SPEC] * 7,
        out_specs=VMEM_SPEC,
        scratch_shapes=[
            vmem((list_len, rows), i32),
            vmem((1, rows), i32),
            vmem((limit, G), i32),
            vmem((rows, 2, width), bf16),
            vmem((2, rows, width), f32),
            vmem((kv_dev, G, rows, per_kv * HEAD_SIZE), bf16),
            vmem((G, m_pad, LANES), f32),
            vmem((T, 8, LANES), i32),
            pltpu.SMEM((T, 8, LANES), i32),
            vmem((G, rows, tokens), f32),
            vmem((tokens, HEAD_SIZE), bf16),
            vmem((tokens, 2 * HEAD_SIZE), bf16),
            vmem((kv_dev, G, *part), f32),
            vmem((kv_dev, G, rows, LANES), f32),
            vmem((kv_dev, G, *part), bf16),
            vmem((kv_dev, G, h_pad, LANES), f32),
            vmem((kv_dev, G, *part), bf16),
            vmem((kv_dev, G, h_pad, LANES), f32),
            vmem((kv_dev, G // 2, *part), bf16),
            vmem((kv_dev, G // 2, h_pad, LANES), f32),
            vmem((kv_dev, rows, LANES), f32),
            vmem((T, out_weight.shape[0], share), bf16),
            vmem((kv_dev, rows, per_kv * HEAD_SIZE), bf16),
            vmem((T, rows, share), f32),
            vmem((pairs, rows, share), bf16),
            vmem((pairs, rows, share), bf16),
            vmem((max(1, pairs - 1), rows, share), bf16),
            vmem((max(1, pairs - 1), rows, share), bf16),
            dma((T + G - 2,)),
            dma((T + G - 2,)),
            dma((2 * kv_dev, T - 1)),
            dma((2 * kv_dev, T - 1)),
            dma((kv_dev, 2, G - 1)),
            dma((kv_dev, 2, G - 1)),
            dma((kv_dev, G, 2)),
            dma((kv_dev, G, 2)),
            dma((kv_dev, G // 2, 2)),
            dma((2, pairs, 2)),
            dma((2, pairs, 2)),
            dma((3 * kv_dev + 5,)),
            dma((T,)),
        ]
        + [vmem((T, pages_dev, page, HEAD_SIZE), bf16)] * (2 * kv_dev),
        compiler_params=pltpu.CompilerParams(
            collective_id=0, has_side_effects=True, vmem_limit_bytes=VMEM_LIMIT
        ),
        name="decode_step",
    )(
        queries, kv_pages, block_table.T, prefix_len.reshape(1, rows),
        fetch_slots.reshape(G, limit).T, newest_key_value, out_weight,
    )


def solution(mesh):
    in_specs = (
        P(("rep", "grp"), "tp"),
        P(("rep", "grp"), None, None),
        P(("rep", "grp", "tp"), None, None, None),
        P("rep", ("grp", "tp"), None),
        P(("rep", "grp"), None),
        P(("rep", "grp")),
        P("tp", None),
    )
    out_specs = P(("rep", "grp"), "tp")
    return jax.shard_map(
        per_device, mesh=mesh, in_specs=in_specs, out_specs=out_specs, check_vma=False
    )
```

```python
import functools
import math

import jax
import jax.numpy as jnp
from jax import lax
from jax.experimental import pallas as pl
from jax.experimental.pallas import tpu as pltpu
from jax.sharding import PartitionSpec as P

QUERY_HEADS = 64
KEY_VALUE_HEADS = 8
HEAD_SIZE = 128
GROUP_WIDTH = QUERY_HEADS // KEY_VALUE_HEADS
DEAD = -1e30
SCALE = math.log2(math.e) / math.sqrt(HEAD_SIZE)
MESH = pl.DeviceIdType.MESH
VMEM_LIMIT = 60 * 1024 * 1024
LANES = 128
RIGHT, LEFT = 0, 1

VMEM_SPEC = pl.BlockSpec(memory_space=pltpu.VMEM)
ANY_SPEC = pl.BlockSpec(memory_space=pl.ANY)


def routes():
    count, me = lax.axis_size("tp"), lax.axis_index("tp")
    pair, core, pairs = me // 2, me % 2, count // 2
    steps = [(i, b) for i in range(1, pairs) for b in range(2)] + [(0, 1)]
    return [(i, b, lax.rem(pair + i, pairs) * 2 + lax.rem(core + b, 2)) for i, b in steps]


def meet():
    barrier = pltpu.get_barrier_semaphore()
    groups, me = lax.axis_size("grp"), lax.axis_index("grp")
    ids = [{"tp": t} for _, _, t in routes()]
    ids += [{"grp": lax.rem(me + d, groups)} for d in range(1, groups)]
    for device in ids:
        pl.semaphore_signal(barrier, inc=1, device_id=device, device_id_type=MESH)
    pl.semaphore_wait(barrier, len(ids))


def remote(source, dest, send_sem, recv_sem, device):
    return pltpu.make_async_remote_copy(
        src_ref=source, dst_ref=dest, send_sem=send_sem, recv_sem=recv_sem,
        device_id=device, device_id_type=MESH,
    )


def turned(tile):
    a = tile.shape[0]
    if a < LANES:
        tile = jnp.concatenate([tile, jnp.zeros((LANES - a, LANES), jnp.float32)], axis=0)
    return tile.T


def weights_of(stats):
    top = functools.reduce(jnp.maximum, stats)
    parts = [jnp.exp2(s - top) for s in stats]
    total = functools.reduce(jnp.add, parts)
    inverse = 1.0 / total
    return [p * inverse for p in parts], top + jnp.log2(total)


def step_kernel(
    limit, q_in, kv_in, table_in, length_in, fetch_in, new_in, w_in, out_ref,
    table_ref, length_ref, fetch_ref, pair_ref, new_ref, q_ref, meta_ref, slots_ref, slots_smem, mask_ref, ksel_ref, vsel_ref,
    o_own, st_own, o_send, st_send, o_mid, st_mid, o_got, st_got, new_st,
    w_ref, mix_ref, acc_ref, core_send, core_got, far_send, far_got,
    small_send, small_recv, kv_send, kv_recv, q_send, q_recv, part_send, mid_recv, got_recv, out_send, out_recv, own_sems, w_sems, *page_refs,
):
    kv_heads, groups, rows, cols = q_ref.shape
    owners, pages_dev, page, _ = page_refs[0].shape
    per_kv = cols // HEAD_SIZE
    heads = per_kv * kv_heads
    list_len = table_ref.shape[0]
    tokens = mask_ref.shape[2]
    pairs = owners // 2
    my_group, my_tp = lax.axis_index("grp"), lax.axis_index("tp")
    share = w_ref.shape[2]
    peers = routes()
    chained = kv_heads - 1

    heads_done = 3 * kv_heads + 1
    first_kv = (my_tp * heads // GROUP_WIDTH) * HEAD_SIZE
    new_cols = pl.ds(pl.multiple_of(first_kv, HEAD_SIZE), kv_heads * HEAD_SIZE)
    loads = [
        pltpu.make_async_copy(source, dest, own_sems.at[heads_done + i])
        for i, (source, dest) in enumerate(
            [
                (table_in, table_ref),
                (length_in, length_ref),
                (fetch_in, fetch_ref),
                (new_in.at[:, :, new_cols], pair_ref),
            ]
        )
    ]
    for load in loads:
        load.start()

    meet()

    small = []
    for i, (_, _, t) in enumerate(peers):
        small.append(
            remote(slots_ref.at[my_tp], slots_ref.at[my_tp], small_send.at[i], small_recv.at[i], {"tp": t})
        )
    for d in range(1, groups):
        i = owners - 2 + d
        small.append(
            remote(
                meta_ref.at[my_group], meta_ref.at[my_group], small_send.at[i], small_recv.at[i],
                {"grp": lax.rem(my_group + d, groups)},
            )
        )
    def q_cols(k):
        return q_in.at[:, k * cols : (k + 1) * cols]

    def q_hop(k, way, d, source=None):
        group = my_group - (d - 1) if way == RIGHT else my_group + (d - 1)
        held = q_ref.at[k, group]
        nbr = my_group + 1 if way == RIGHT else my_group - 1
        return remote(
            held if source is None else source, held,
            q_send.at[k, way, d - 1], q_recv.at[k, way, d - 1], {"grp": nbr},
        )

    def can_send(way, d):
        if way == RIGHT:
            return (my_group + 1 < groups) & (my_group - (d - 1) >= 0)
        return (my_group >= 1) & (my_group + (d - 1) < groups)

    def can_get(way, d):
        return my_group - d >= 0 if way == RIGHT else my_group + d < groups

    def q_arrived(k, way, d):
        group = my_group - d if way == RIGHT else my_group + d
        held = q_ref.at[k, group]
        nbr = my_group - 1 if way == RIGHT else my_group + 1
        return remote(held, held, q_send.at[k, way, d - 1], q_recv.at[k, way, d - 1], {"grp": nbr})

    def own_q(k):
        return pltpu.make_async_copy(q_cols(k), q_ref.at[k, my_group], own_sems.at[k])

    def kv_columns(k, kind, t):
        first = (t * heads // GROUP_WIDTH + k) * HEAD_SIZE
        return kv_in.at[:, kind, :, pl.ds(pl.multiple_of(first, HEAD_SIZE), HEAD_SIZE)]

    def kv_copies(k, kind):
        n = 2 * k + kind
        dest = page_refs[n].at[my_tp]
        copies = [
            remote(kv_columns(k, kind, t), dest, kv_send.at[n, i], kv_recv.at[n, i], {"tp": t})
            for i, (_, _, t) in enumerate(peers)
        ]
        copies.append(
            pltpu.make_async_copy(kv_columns(k, kind, my_tp), dest, own_sems.at[kv_heads + n])
        )
        return copies

    def far_copy(k, kind, i, core):
        n = 2 * k + kind
        slot = 2 * (i - 1) + lax.rem(core + my_tp, 2)
        t = lax.rem(my_tp // 2 + i, pairs) * 2 + core
        return remote(
            kv_columns(k, kind, t), page_refs[n].at[my_tp], kv_send.at[n, slot], kv_recv.at[n, slot],
            {"tp": t},
        )

    def first_things():
        for load in loads:
            load.wait()
        meta_ref[my_group] = jnp.zeros(meta_ref.shape[1:], jnp.float32)
        meta_ref[my_group, :list_len, :rows] = table_ref[...].astype(jnp.float32)
        meta_ref[my_group, list_len : list_len + 1, :rows] = length_ref[...].astype(jnp.float32)
        slots_ref[my_tp] = jnp.zeros(slots_ref.shape[1:], jnp.int32)
        slots_ref[my_tp, :limit, :groups] = fetch_ref[...]
        for copy in small:
            copy.start()

    kv_all = {(k, kind): kv_copies(k, kind) for k in range(kv_heads) for kind in range(2)}
    for k in range(kv_heads):
        for way in (RIGHT, LEFT):
            pl.when(can_send(way, 1))(lambda k=k, way=way: q_hop(k, way, 1, q_cols(k)).start())
        for core in range(2):
            for kind in range(2):
                for i in range(1, pairs):
                    far_copy(k, kind, i, core).start()
            if k == 0 and core == 0:
                first_things()
        for kind in range(2):
            for copy in kv_all[k, kind][2 * (pairs - 1) :]:
                copy.start()
        own_q(k).start()

    slot_ids = [(i, b, t) for i, b, t in peers] + [(0, 0, my_tp)]
    w_copies = []
    for s, (_, _, t) in enumerate(slot_ids):
        span = pl.ds(pl.multiple_of(t * share, 128), share)
        w_copies.append(pltpu.make_async_copy(w_in.at[:, span], w_ref.at[s], w_sems.at[s]))
        w_copies[-1].start()

    vsel_ref[:, HEAD_SIZE:] = jnp.ones((tokens, HEAD_SIZE), jnp.bfloat16)

    for copy in small:
        copy.wait_recv()
    to_smem = pltpu.make_async_copy(slots_ref, slots_smem, own_sems.at[3 * kv_heads])
    to_smem.start()

    def relay(k, d):
        for way in (RIGHT, LEFT):

            @pl.when(can_get(way, d))
            def _():
                q_arrived(k, way, d).wait_recv()

            if d < groups - 1:
                pl.when(can_send(way, d + 1))(lambda: q_hop(k, way, d + 1).start())

    lane_p = lax.broadcasted_iota(jnp.int32, (rows, page), 1)
    lane_j = lax.broadcasted_iota(jnp.int32, (rows, list_len), 1)

    def build(g, carry):
        both = turned(meta_ref[g])[:rows].astype(jnp.int32)
        entries = both[:, :list_len]
        length = both[:, list_len : list_len + 1]
        full, tail = length // page, length % page
        for n in range(owners * limit):
            same = entries == my_group * owners * limit + n
            whole = jnp.sum(jnp.where(same & (lane_j < full), 1.0, 0.0), axis=1, keepdims=True)
            part = jnp.sum(jnp.where(same & (lane_j == full), 1.0, 0.0), axis=1, keepdims=True)
            count = whole + jnp.where(lane_p < tail, part, 0.0)
            mask_ref[g, :, n * page : (n + 1) * page] = jnp.where(
                count > 0.0, jnp.log2(jnp.maximum(count, 1.0)), DEAD
            )
        return carry


    lane_s = lax.broadcasted_iota(jnp.int32, (rows, LANES), 1)
    unroll = 2 if per_kv % 2 == 0 else 1

    def attend(k, g):
        for n in range(owners * limit):
            t, c = n // limit, n % limit
            slot = jnp.maximum(slots_smem[t, c, g], 0)
            span = slice(n * page, (n + 1) * page)
            ksel_ref[span] = page_refs[2 * k][t, slot]
            vsel_ref[span, :HEAD_SIZE] = page_refs[2 * k + 1][t, slot]
        stats = jnp.zeros((rows, LANES), jnp.float32)
        sums = jnp.ones((rows, LANES), jnp.float32)
        for h0 in range(0, per_kv, unroll):
            q = jnp.concatenate(
                [
                    q_ref[k, g, :, h * HEAD_SIZE : (h + 1) * HEAD_SIZE]
                    for h in range(h0, h0 + unroll)
                ],
                axis=0,
            )
            s = lax.dot_general(
                q, ksel_ref[...], (((1,), (1,)), ((), ())), preferred_element_type=jnp.float32
            )
            s = s.reshape(unroll, rows, tokens) * SCALE + mask_ref[g][None]
            top = jnp.max(s, axis=2, keepdims=True)
            e = jnp.exp2(s - top).astype(jnp.bfloat16).reshape(unroll * rows, tokens)
            mixed = jnp.dot(e, vsel_ref[...], preferred_element_type=jnp.float32)
            total = mixed[:, HEAD_SIZE:]
            out = mixed[:, :HEAD_SIZE] / total
            span = slice(h0 * rows, (h0 + unroll) * rows)
            o_own[k, g, span] = out
            o_send[k, g, span] = out.astype(jnp.bfloat16)
            for u in range(unroll):
                here = lane_s == h0 + u
                stats = jnp.where(here, top[u], stats)
                sums = jnp.where(here, total[u * rows : (u + 1) * rows], sums)
        stats = stats + jnp.log2(sums)
        st_own[k, g] = stats
        st_send[k, g] = turned(stats)[: st_send.shape[2]]

    pair = my_group // 2
    neighbour = my_group + 1 - 2 * lax.rem(my_group, 2)

    def carried(g):
        return (g // 2 != pair) & ((g > my_group) == (lax.rem(my_group, 2) == 1))

    def to_mid(k, g):
        return [
            remote(o_send.at[k, g], o_mid.at[k, g], part_send.at[k, g, 0], mid_recv.at[k, g, 0], {"grp": neighbour}),
            remote(st_send.at[k, g], st_mid.at[k, g], part_send.at[k, g, 1], mid_recv.at[k, g, 1], {"grp": neighbour}),
        ]

    def to_end(k, g, group):
        return [
            remote(o_send.at[k, g], o_got.at[k, pair], part_send.at[k, g, 0], got_recv.at[k, pair, 0], {"grp": group}),
            remote(st_send.at[k, g], st_got.at[k, pair], part_send.at[k, g, 1], got_recv.at[k, pair, 1], {"grp": group}),
        ]

    def from_pair(k, n):
        return [
            remote(o_got.at[k, n], o_got.at[k, n], part_send.at[k, 0, 0], got_recv.at[k, n, 0], {"grp": neighbour}),
            remote(st_got.at[k, n], st_got.at[k, n], part_send.at[k, 0, 1], got_recv.at[k, n, 1], {"grp": neighbour}),
        ]

    def place(j):
        d = (j + 1) // 2
        left = lax.rem(j, 2) == 1
        g = jnp.where(left, my_group - d, my_group + d)
        return d, left, g, (g >= 0) & (g < groups)

    def attend_some(k, first, last, far=False):
        low, high = max(0, 2 * first - 1), 2 * last + 1

        def body(i, carry):
            d, left, g, valid = place(low + high - 1 - i if far else i)

            @pl.when(valid)
            def _():
                if groups > 1:

                    @pl.when((d == groups - 1) & left)
                    def _():
                        q_arrived(k, RIGHT, groups - 1).wait_recv()

                    @pl.when((d == groups - 1) & jnp.logical_not(left))
                    def _():
                        q_arrived(k, LEFT, groups - 1).wait_recv()

                attend(k, g)

                @pl.when(g == neighbour)
                def _():
                    for copy in to_end(k, g, neighbour):
                        copy.start()

                @pl.when((g // 2 != pair) & jnp.logical_not(carried(g)))
                def _():
                    for copy in to_mid(k, g):
                        copy.start()

            return carry

        lax.fori_loop(low, high, body, 0)

    def spread_stats(tile):
        tile = jnp.concatenate(
            [tile, jnp.zeros((LANES - tile.shape[0], LANES), jnp.float32)], axis=0
        )
        return tile.T[:rows]

    def head_rows(h):
        return slice(h * rows, (h + 1) * rows)

    def pass_on(k, before, after, far=True):
        def body(i, carry):
            _, _, g, valid = place(2 * groups - 2 - i if far else i + 1)
            before(i)

            @pl.when(valid & carried(g))
            def _():
                for copy in to_mid(k, g):
                    copy.wait_recv()
                (mine, other), level = weights_of([st_own[k, g], spread_stats(st_mid[k, g])])
                for h in range(per_kv):
                    out = mine[:, h : h + 1] * o_own[k, g, head_rows(h)]
                    out += other[:, h : h + 1] * o_mid[k, g, head_rows(h)].astype(jnp.float32)
                    o_send[k, g, head_rows(h)] = out.astype(jnp.bfloat16)
                st_send[k, g] = turned(level)[: st_send.shape[2]]
                for copy in to_end(k, g, g):
                    copy.start()

            after(i)
            return carry

        lax.fori_loop(0, 2 * groups - 2, body, 0)

    def finish(k):
        others = [o_got.at[k, n] for n in range(groups // 2)]
        for n in range(groups // 2):
            for copy in from_pair(k, n):
                copy.wait_recv()
        levels = [spread_stats(st_got[k, n]) for n in range(groups // 2)]
        stats = [st_own[k, my_group], new_st[k]] + levels
        ways, _ = weights_of(stats)
        new_value = new_ref[1, :, k * HEAD_SIZE : (k + 1) * HEAD_SIZE]
        for h in range(per_kv):
            out = ways[0][:, h : h + 1] * o_own[k, my_group, head_rows(h)]
            out += ways[1][:, h : h + 1] * new_value
            for way, ref in zip(ways[2:], others):
                out += way[:, h : h + 1] * ref[head_rows(h)].astype(jnp.float32)
            mix_ref[k, :, h * HEAD_SIZE : (h + 1) * HEAD_SIZE] = out.astype(jnp.bfloat16)

    halves = max(n for n in (1, 2, 4) if share % (n * 128) == 0)
    half = share // halves
    block = half

    def project(k, s, part):
        def body(n, carry):
            span = pl.ds(pl.multiple_of(part * half + n * block, 128), block)
            made = jnp.dot(
                mix_ref[k], w_ref[s, k * cols : (k + 1) * cols, span],
                preferred_element_type=jnp.float32,
            )
            acc_ref[s, :, span] = made if k == 0 else acc_ref[s, :, span] + made
            return carry

        lax.fori_loop(0, half // block, body, 0)

    def nothing(i):
        pass

    def new_token():
        both = pair_ref[...].astype(jnp.float32)
        which = lax.broadcasted_iota(jnp.int32, both.shape, 1)
        for kind in range(2):
            new_ref[kind] = jnp.sum(jnp.where(which == kind, both, 0.0), axis=1)
        for k in range(kv_heads):
            own_q(k).wait()
            new_key = new_ref[0, :, k * HEAD_SIZE : (k + 1) * HEAD_SIZE]
            lane = lax.broadcasted_iota(jnp.int32, (rows, LANES), 1)
            tile = jnp.zeros((rows, LANES), jnp.float32)
            for h in range(per_kv):
                q = q_ref[k, my_group, :, h * HEAD_SIZE : (h + 1) * HEAD_SIZE].astype(jnp.float32)
                tile = jnp.where(lane == h, jnp.sum(q * new_key, axis=1, keepdims=True) * SCALE, tile)
            new_st[k] = tile

    def kv_arrived(k):
        for kind in range(2):
            for copy in kv_all[k, kind][:-1]:
                copy.wait_recv()
            kv_all[k, kind][-1].wait()

    def whole(k, s):
        for part in range(halves):
            project(k, s, part)

    core = lax.rem(my_tp, 2)

    def hop(d, heads_of):
        if d < groups - 1:
            for k in heads_of:
                relay(k, d)

    hop(1, [0])
    lax.fori_loop(0, groups // 2, build, 0)
    hop(1, range(1, kv_heads))
    lax.fori_loop(groups // 2, groups, build, 0)
    to_smem.wait()
    new_token()

    reach = min(1, groups - 1)

    @pl.when(core == 0)
    def _():
        kv_arrived(0)
        attend_some(0, 0, reach)

    hop(2, [0])

    @pl.when(core == 1)
    def _():
        kv_arrived(0)
        attend_some(0, 0, reach)

    hop(2, range(1, kv_heads))
    for d in range(2, groups):
        if d > 2:
            hop(d, range(kv_heads))
        attend_some(0, d, d)

    def ahead(k):
        pass_on(k, nothing, nothing, far=False)

    def catch_up(k):
        kv_arrived(k)
        attend_some(k, 0, groups - 1, far=True)

    for k in range(1, kv_heads):

        @pl.when(core == 0)
        def _():
            catch_up(k)
            ahead(k - 1)

        @pl.when(core == 1)
        def _():
            ahead(k - 1)
            catch_up(k)

    for copy in w_copies:
        copy.wait()

    pass_on(chained, nothing, nothing)
    for k in range(chained):
        finish(k)
        for s in range(owners):
            whole(k, s)

    finish(chained)

    mate = {"tp": my_tp + 1 - 2 * lax.rem(my_tp, 2)}
    cores, fars = {}, {}

    def last(s, span):
        made = jnp.dot(
            mix_ref[chained], w_ref[s, chained * cols : (chained + 1) * cols, span],
            preferred_element_type=jnp.float32,
        )
        return made if chained == 0 else acc_ref[s, :, span] + made

    index = {(i, b): s for s, (i, b, _) in enumerate(slot_ids)}
    spans = [slice(p * half, (p + 1) * half) for p in range(halves)]
    for i in range(pairs):
        for p, span in enumerate(spans):
            cores[i, p] = remote(
                core_send.at[i, :, span], core_got.at[i, :, span],
                out_send.at[0, i, p], out_recv.at[0, i, p], mate,
            )
            if i > 0:
                fars[i, p] = remote(
                    far_send.at[i - 1, :, span], far_got.at[i - 1, :, span],
                    out_send.at[1, i, p], out_recv.at[1, i, p], {"tp": slot_ids[index[i, 0]][2]},
                )

    def to_mate(i, p):
        span = spans[p]
        core_send[i, :, span] = last(index[i, 1], span).astype(jnp.bfloat16)
        cores[i, p].start()

    def to_far(i, p):
        span = spans[p]
        made = last(index[i, 0], span)
        if i == 0:
            acc_ref[index[0, 0], :, span] = made
        else:
            cores[i, p].wait_recv()
            far_send[i - 1, :, span] = (
                made + core_got[i, :, span].astype(jnp.float32)
            ).astype(jnp.bfloat16)
            fars[i, p].start()

    @pl.when(core == 0)
    def _():
        for i in list(range(1, pairs)) + [0]:
            for p in range(halves):
                to_mate(i, p)
        for i in list(range(1, pairs)) + [0]:
            for p in range(halves):
                to_far(i, p)

    @pl.when(core == 1)
    def _():
        for i in list(range(1, pairs)) + [0]:
            for p in range(halves):
                to_far(i, p)
                to_mate(i, p)

    for p, span in enumerate(spans):
        cores[0, p].wait_recv()
        total = acc_ref[index[0, 0], :, span] + core_got[0, :, span].astype(jnp.float32)
        for i in range(1, pairs):
            fars[i, p].wait_recv()
            total = total + far_got[i - 1, :, span].astype(jnp.float32)
        out_ref[:, span] = total.astype(jnp.bfloat16)

    sent = small + list(cores.values()) + list(fars.values())
    for copies in kv_all.values():
        sent += copies[:-1]
    for copy in sent:
        copy.wait_send()
    for k in range(kv_heads):
        for d in range(1, groups):
            for way in (RIGHT, LEFT):
                source = q_cols(k) if d == 1 else None
                pl.when(can_send(way, d))(lambda: q_hop(k, way, d, source).wait_send())
    for k in range(kv_heads):
        for g in range(groups):

            @pl.when(my_group != g)
            def _():
                for copy in to_mid(k, g):
                    copy.wait_send()


def per_device(
    queries, newest_key_value, kv_pages, fetch_slots, block_table, prefix_len, out_weight
):
    T = lax.axis_size("tp")
    G = lax.axis_size("grp")
    rows, cols = queries.shape
    heads = cols // HEAD_SIZE
    kv_dev = max(1, heads // GROUP_WIDTH)
    per_kv = heads // kv_dev
    width = kv_dev * HEAD_SIZE
    pages_dev, _, page, _ = kv_pages.shape
    list_len = block_table.shape[1]
    limit = fetch_slots.shape[2]
    model = out_weight.shape[1]
    dma = pltpu.SemaphoreType.DMA

    share = model // T
    pairs = T // 2
    bf16, f32, i32 = jnp.bfloat16, jnp.float32, jnp.int32
    vmem = pltpu.VMEM
    h_pad = -(-per_kv // 8) * 8
    m_pad = -(-(list_len + 1) // 8) * 8
    tokens = T * limit * page
    part = (per_kv * rows, HEAD_SIZE)
    return pl.pallas_call(
        functools.partial(step_kernel, limit),
        out_shape=jax.ShapeDtypeStruct((rows, share), bf16),
        in_specs=[ANY_SPEC] * 7,
        out_specs=VMEM_SPEC,
        scratch_shapes=[
            vmem((list_len, rows), i32),
            vmem((1, rows), i32),
            vmem((limit, G), i32),
            vmem((rows, 2, width), bf16),
            vmem((2, rows, width), f32),
            vmem((kv_dev, G, rows, per_kv * HEAD_SIZE), bf16),
            vmem((G, m_pad, LANES), f32),
            vmem((T, 8, LANES), i32),
            pltpu.SMEM((T, 8, LANES), i32),
            vmem((G, rows, tokens), f32),
            vmem((tokens, HEAD_SIZE), bf16),
            vmem((tokens, 2 * HEAD_SIZE), bf16),
            vmem((kv_dev, G, *part), f32),
            vmem((kv_dev, G, rows, LANES), f32),
            vmem((kv_dev, G, *part), bf16),
            vmem((kv_dev, G, h_pad, LANES), f32),
            vmem((kv_dev, G, *part), bf16),
            vmem((kv_dev, G, h_pad, LANES), f32),
            vmem((kv_dev, G // 2, *part), bf16),
            vmem((kv_dev, G // 2, h_pad, LANES), f32),
            vmem((kv_dev, rows, LANES), f32),
            vmem((T, out_weight.shape[0], share), bf16),
            vmem((kv_dev, rows, per_kv * HEAD_SIZE), bf16),
            vmem((T, rows, share), f32),
            vmem((pairs, rows, share), bf16),
            vmem((pairs, rows, share), bf16),
            vmem((max(1, pairs - 1), rows, share), bf16),
            vmem((max(1, pairs - 1), rows, share), bf16),
            dma((T + G - 2,)),
            dma((T + G - 2,)),
            dma((2 * kv_dev, T - 1)),
            dma((2 * kv_dev, T - 1)),
            dma((kv_dev, 2, G - 1)),
            dma((kv_dev, 2, G - 1)),
            dma((kv_dev, G, 2)),
            dma((kv_dev, G, 2)),
            dma((kv_dev, G // 2, 2)),
            dma((2, pairs, 4)),
            dma((2, pairs, 4)),
            dma((3 * kv_dev + 5,)),
            dma((T,)),
        ]
        + [vmem((T, pages_dev, page, HEAD_SIZE), bf16)] * (2 * kv_dev),
        compiler_params=pltpu.CompilerParams(
            collective_id=0, has_side_effects=True, vmem_limit_bytes=VMEM_LIMIT
        ),
        name="decode_step",
    )(
        queries, kv_pages, block_table.T, prefix_len.reshape(1, rows),
        fetch_slots.reshape(G, limit).T, newest_key_value, out_weight,
    )


def solution(mesh):
    in_specs = (
        P(("rep", "grp"), "tp"),
        P(("rep", "grp"), None, None),
        P(("rep", "grp", "tp"), None, None, None),
        P("rep", ("grp", "tp"), None),
        P(("rep", "grp"), None),
        P(("rep", "grp")),
        P("tp", None),
    )
    out_specs = P(("rep", "grp"), "tp")
    return jax.shard_map(
        per_device, mesh=mesh, in_specs=in_specs, out_specs=out_specs, check_vma=False
    )
```

```python
import functools
import math

import jax
import jax.numpy as jnp
from jax import lax
from jax.experimental import pallas as pl
from jax.experimental.pallas import tpu as pltpu
from jax.sharding import PartitionSpec as P

QUERY_HEADS = 64
KEY_VALUE_HEADS = 8
HEAD_SIZE = 128
GROUP_WIDTH = QUERY_HEADS // KEY_VALUE_HEADS
DEAD = -1e30
SCALE = math.log2(math.e) / math.sqrt(HEAD_SIZE)
MESH = pl.DeviceIdType.MESH
VMEM_LIMIT = 60 * 1024 * 1024
LANES = 128
RIGHT, LEFT = 0, 1

VMEM_SPEC = pl.BlockSpec(memory_space=pltpu.VMEM)
ANY_SPEC = pl.BlockSpec(memory_space=pl.ANY)


def routes():
    count, me = lax.axis_size("tp"), lax.axis_index("tp")
    pair, core, pairs = me // 2, me % 2, count // 2
    steps = [(i, b) for i in range(1, pairs) for b in range(2)] + [(0, 1)]
    return [(i, b, lax.rem(pair + i, pairs) * 2 + lax.rem(core + b, 2)) for i, b in steps]


def meet():
    barrier = pltpu.get_barrier_semaphore()
    groups, me = lax.axis_size("grp"), lax.axis_index("grp")
    ids = [{"tp": t} for _, _, t in routes()]
    ids += [{"grp": lax.rem(me + d, groups)} for d in range(1, groups)]
    for device in ids:
        pl.semaphore_signal(barrier, inc=1, device_id=device, device_id_type=MESH)
    pl.semaphore_wait(barrier, len(ids))


def remote(source, dest, send_sem, recv_sem, device):
    return pltpu.make_async_remote_copy(
        src_ref=source, dst_ref=dest, send_sem=send_sem, recv_sem=recv_sem,
        device_id=device, device_id_type=MESH,
    )


def turned(tile):
    a = tile.shape[0]
    if a < LANES:
        tile = jnp.concatenate([tile, jnp.zeros((LANES - a, LANES), jnp.float32)], axis=0)
    return tile.T


def weights_of(stats):
    top = functools.reduce(jnp.maximum, stats)
    parts = [jnp.exp2(s - top) for s in stats]
    total = functools.reduce(jnp.add, parts)
    inverse = 1.0 / total
    return [p * inverse for p in parts], top + jnp.log2(total)


def step_kernel(
    limit, q_in, kv_in, table_in, length_in, fetch_in, new_in, w_in, out_ref,
    table_ref, length_ref, fetch_ref, pair_ref, new_ref, q_ref, meta_ref, slots_ref, slots_smem, mask_ref, ksel_ref, vsel_ref,
    o_own, st_own, o_send, st_send, o_mid, st_mid, o_got, st_got, new_st,
    w_ref, mix_ref, acc_ref, core_send, core_got, far_send, far_got,
    small_send, small_recv, kv_send, kv_recv, q_send, q_recv, part_send, mid_recv, got_recv, out_send, out_recv, own_sems, w_sems, *page_refs,
):
    kv_heads, groups, rows, cols = q_ref.shape
    owners, pages_dev, page, _ = page_refs[0].shape
    per_kv = cols // HEAD_SIZE
    heads = per_kv * kv_heads
    list_len = table_ref.shape[0]
    tokens = mask_ref.shape[2]
    pairs = owners // 2
    my_group, my_tp = lax.axis_index("grp"), lax.axis_index("tp")
    share = w_ref.shape[2]
    peers = routes()
    chained = kv_heads - 1

    heads_done = 3 * kv_heads + 1
    first_kv = (my_tp * heads // GROUP_WIDTH) * HEAD_SIZE
    new_cols = pl.ds(pl.multiple_of(first_kv, HEAD_SIZE), kv_heads * HEAD_SIZE)
    loads = [
        pltpu.make_async_copy(source, dest, own_sems.at[heads_done + i])
        for i, (source, dest) in enumerate(
            [
                (table_in, table_ref),
                (length_in, length_ref),
                (fetch_in, fetch_ref),
                (new_in.at[:, :, new_cols], pair_ref),
            ]
        )
    ]
    for load in loads:
        load.start()

    meet()

    small = []
    for i, (_, _, t) in enumerate(peers):
        small.append(
            remote(slots_ref.at[my_tp], slots_ref.at[my_tp], small_send.at[i], small_recv.at[i], {"tp": t})
        )
    for d in range(1, groups):
        i = owners - 2 + d
        small.append(
            remote(
                meta_ref.at[my_group], meta_ref.at[my_group], small_send.at[i], small_recv.at[i],
                {"grp": lax.rem(my_group + d, groups)},
            )
        )
    def q_cols(k):
        return q_in.at[:, k * cols : (k + 1) * cols]

    def q_hop(k, way, d, source=None):
        group = my_group - (d - 1) if way == RIGHT else my_group + (d - 1)
        held = q_ref.at[k, group]
        nbr = my_group + 1 if way == RIGHT else my_group - 1
        return remote(
            held if source is None else source, held,
            q_send.at[k, way, d - 1], q_recv.at[k, way, d - 1], {"grp": nbr},
        )

    def can_send(way, d):
        if way == RIGHT:
            return (my_group + 1 < groups) & (my_group - (d - 1) >= 0)
        return (my_group >= 1) & (my_group + (d - 1) < groups)

    def can_get(way, d):
        return my_group - d >= 0 if way == RIGHT else my_group + d < groups

    def q_arrived(k, way, d):
        group = my_group - d if way == RIGHT else my_group + d
        held = q_ref.at[k, group]
        nbr = my_group - 1 if way == RIGHT else my_group + 1
        return remote(held, held, q_send.at[k, way, d - 1], q_recv.at[k, way, d - 1], {"grp": nbr})

    def own_q(k):
        return pltpu.make_async_copy(q_cols(k), q_ref.at[k, my_group], own_sems.at[k])

    def kv_columns(k, kind, t):
        first = (t * heads // GROUP_WIDTH + k) * HEAD_SIZE
        return kv_in.at[:, kind, :, pl.ds(pl.multiple_of(first, HEAD_SIZE), HEAD_SIZE)]

    def kv_copies(k, kind):
        n = 2 * k + kind
        dest = page_refs[n].at[my_tp]
        copies = [
            remote(kv_columns(k, kind, t), dest, kv_send.at[n, i], kv_recv.at[n, i], {"tp": t})
            for i, (_, _, t) in enumerate(peers)
        ]
        copies.append(
            pltpu.make_async_copy(kv_columns(k, kind, my_tp), dest, own_sems.at[kv_heads + n])
        )
        return copies

    def far_copy(k, kind, i, core):
        n = 2 * k + kind
        slot = 2 * (i - 1) + lax.rem(core + my_tp, 2)
        t = lax.rem(my_tp // 2 + i, pairs) * 2 + core
        return remote(
            kv_columns(k, kind, t), page_refs[n].at[my_tp], kv_send.at[n, slot], kv_recv.at[n, slot],
            {"tp": t},
        )

    def first_things():
        for load in loads:
            load.wait()
        meta_ref[my_group] = jnp.zeros(meta_ref.shape[1:], jnp.float32)
        meta_ref[my_group, :list_len, :rows] = table_ref[...].astype(jnp.float32)
        meta_ref[my_group, list_len : list_len + 1, :rows] = length_ref[...].astype(jnp.float32)
        slots_ref[my_tp] = jnp.zeros(slots_ref.shape[1:], jnp.int32)
        slots_ref[my_tp, :limit, :groups] = fetch_ref[...]
        for copy in small:
            copy.start()

    kv_all = {(k, kind): kv_copies(k, kind) for k in range(kv_heads) for kind in range(2)}
    for k in range(kv_heads):
        for way in (RIGHT, LEFT):
            pl.when(can_send(way, 1))(lambda k=k, way=way: q_hop(k, way, 1, q_cols(k)).start())
        for core in range(2):
            for kind in range(2):
                for i in range(1, pairs):
                    far_copy(k, kind, i, core).start()
            if k == 0 and core == 0:
                first_things()
        for kind in range(2):
            for copy in kv_all[k, kind][2 * (pairs - 1) :]:
                copy.start()
        own_q(k).start()

    slot_ids = [(i, b, t) for i, b, t in peers] + [(0, 0, my_tp)]
    w_copies = []
    for s, (_, _, t) in enumerate(slot_ids):
        span = pl.ds(pl.multiple_of(t * share, 128), share)
        w_copies.append(pltpu.make_async_copy(w_in.at[:, span], w_ref.at[s], w_sems.at[s]))
        w_copies[-1].start()

    vsel_ref[:, HEAD_SIZE:] = jnp.ones((tokens, HEAD_SIZE), jnp.bfloat16)

    for copy in small:
        copy.wait_recv()
    to_smem = pltpu.make_async_copy(slots_ref, slots_smem, own_sems.at[3 * kv_heads])
    to_smem.start()

    def relay(k, d):
        for way in (RIGHT, LEFT):

            @pl.when(can_get(way, d))
            def _():
                q_arrived(k, way, d).wait_recv()

            if d < groups - 1:
                pl.when(can_send(way, d + 1))(lambda: q_hop(k, way, d + 1).start())

    lane_p = lax.broadcasted_iota(jnp.int32, (rows, page), 1)
    lane_j = lax.broadcasted_iota(jnp.int32, (rows, list_len), 1)

    def build(g, carry):
        both = turned(meta_ref[g])[:rows].astype(jnp.int32)
        entries = both[:, :list_len]
        length = both[:, list_len : list_len + 1]
        full, tail = length // page, length % page
        for n in range(owners * limit):
            same = entries == my_group * owners * limit + n
            whole = jnp.sum(jnp.where(same & (lane_j < full), 1.0, 0.0), axis=1, keepdims=True)
            part = jnp.sum(jnp.where(same & (lane_j == full), 1.0, 0.0), axis=1, keepdims=True)
            count = whole + jnp.where(lane_p < tail, part, 0.0)
            mask_ref[g, :, n * page : (n + 1) * page] = jnp.where(
                count > 0.0, jnp.log2(jnp.maximum(count, 1.0)), DEAD
            )
        return carry


    lane_s = lax.broadcasted_iota(jnp.int32, (rows, LANES), 1)
    unroll = 4 if per_kv % 4 == 0 else 1

    def attend(k, g):
        for n in range(owners * limit):
            t, c = n // limit, n % limit
            slot = jnp.maximum(slots_smem[t, c, g], 0)
            span = slice(n * page, (n + 1) * page)
            ksel_ref[span] = page_refs[2 * k][t, slot]
            vsel_ref[span, :HEAD_SIZE] = page_refs[2 * k + 1][t, slot]
        stats = jnp.zeros((rows, LANES), jnp.float32)
        sums = jnp.ones((rows, LANES), jnp.float32)
        for h0 in range(0, per_kv, unroll):
            q = jnp.concatenate(
                [
                    q_ref[k, g, :, h * HEAD_SIZE : (h + 1) * HEAD_SIZE]
                    for h in range(h0, h0 + unroll)
                ],
                axis=0,
            )
            s = lax.dot_general(
                q, ksel_ref[...], (((1,), (1,)), ((), ())), preferred_element_type=jnp.float32
            )
            s = s.reshape(unroll, rows, tokens) * SCALE + mask_ref[g][None]
            top = jnp.max(s, axis=2, keepdims=True)
            e = jnp.exp2(s - top).astype(jnp.bfloat16).reshape(unroll * rows, tokens)
            mixed = jnp.dot(e, vsel_ref[...], preferred_element_type=jnp.float32)
            total = mixed[:, HEAD_SIZE:]
            out = mixed[:, :HEAD_SIZE] / total
            span = slice(h0 * rows, (h0 + unroll) * rows)
            o_own[k, g, span] = out
            o_send[k, g, span] = out.astype(jnp.bfloat16)
            for u in range(unroll):
                here = lane_s == h0 + u
                stats = jnp.where(here, top[u], stats)
                sums = jnp.where(here, total[u * rows : (u + 1) * rows], sums)
        stats = stats + jnp.log2(sums)
        st_own[k, g] = stats
        st_send[k, g] = turned(stats)[: st_send.shape[2]]

    pair = my_group // 2
    neighbour = my_group + 1 - 2 * lax.rem(my_group, 2)

    def carried(g):
        return (g // 2 != pair) & ((g > my_group) == (lax.rem(my_group, 2) == 1))

    def to_mid(k, g):
        return [
            remote(o_send.at[k, g], o_mid.at[k, g], part_send.at[k, g, 0], mid_recv.at[k, g, 0], {"grp": neighbour}),
            remote(st_send.at[k, g], st_mid.at[k, g], part_send.at[k, g, 1], mid_recv.at[k, g, 1], {"grp": neighbour}),
        ]

    def to_end(k, g, group):
        return [
            remote(o_send.at[k, g], o_got.at[k, pair], part_send.at[k, g, 0], got_recv.at[k, pair, 0], {"grp": group}),
            remote(st_send.at[k, g], st_got.at[k, pair], part_send.at[k, g, 1], got_recv.at[k, pair, 1], {"grp": group}),
        ]

    def from_pair(k, n):
        return [
            remote(o_got.at[k, n], o_got.at[k, n], part_send.at[k, 0, 0], got_recv.at[k, n, 0], {"grp": neighbour}),
            remote(st_got.at[k, n], st_got.at[k, n], part_send.at[k, 0, 1], got_recv.at[k, n, 1], {"grp": neighbour}),
        ]

    def place(j):
        d = (j + 1) // 2
        left = lax.rem(j, 2) == 1
        g = jnp.where(left, my_group - d, my_group + d)
        return d, left, g, (g >= 0) & (g < groups)

    def attend_some(k, first, last, far=False):
        low, high = max(0, 2 * first - 1), 2 * last + 1

        def body(i, carry):
            d, left, g, valid = place(low + high - 1 - i if far else i)

            @pl.when(valid)
            def _():
                if groups > 1:

                    @pl.when((d == groups - 1) & left)
                    def _():
                        q_arrived(k, RIGHT, groups - 1).wait_recv()

                    @pl.when((d == groups - 1) & jnp.logical_not(left))
                    def _():
                        q_arrived(k, LEFT, groups - 1).wait_recv()

                attend(k, g)

                @pl.when(g == neighbour)
                def _():
                    for copy in reversed(to_end(k, g, neighbour)):
                        copy.start()

                @pl.when((g // 2 != pair) & jnp.logical_not(carried(g)))
                def _():
                    for copy in reversed(to_mid(k, g)):
                        copy.start()

            return carry

        lax.fori_loop(low, high, body, 0)

    def spread_stats(tile):
        tile = jnp.concatenate(
            [tile, jnp.zeros((LANES - tile.shape[0], LANES), jnp.float32)], axis=0
        )
        return tile.T[:rows]

    def head_rows(h):
        return slice(h * rows, (h + 1) * rows)

    def pass_on(k, before, after, far=True):
        def body(i, carry):
            _, _, g, valid = place(2 * groups - 2 - i if far else i + 1)
            before(i)

            @pl.when(valid & carried(g))
            def _():
                for copy in to_mid(k, g):
                    copy.wait_recv()
                (mine, other), level = weights_of([st_own[k, g], spread_stats(st_mid[k, g])])
                for h in range(per_kv):
                    out = mine[:, h : h + 1] * o_own[k, g, head_rows(h)]
                    out += other[:, h : h + 1] * o_mid[k, g, head_rows(h)].astype(jnp.float32)
                    o_send[k, g, head_rows(h)] = out.astype(jnp.bfloat16)
                st_send[k, g] = turned(level)[: st_send.shape[2]]
                for copy in reversed(to_end(k, g, g)):
                    copy.start()

            after(i)
            return carry

        lax.fori_loop(0, 2 * groups - 2, body, 0)

    def finish(k):
        others = [o_got.at[k, n] for n in range(groups // 2)]
        for n in range(groups // 2):
            for copy in from_pair(k, n):
                copy.wait_recv()
        levels = [spread_stats(st_got[k, n]) for n in range(groups // 2)]
        stats = [st_own[k, my_group], new_st[k]] + levels
        ways, _ = weights_of(stats)
        new_value = new_ref[1, :, k * HEAD_SIZE : (k + 1) * HEAD_SIZE]
        for h in range(per_kv):
            out = ways[0][:, h : h + 1] * o_own[k, my_group, head_rows(h)]
            out += ways[1][:, h : h + 1] * new_value
            for way, ref in zip(ways[2:], others):
                out += way[:, h : h + 1] * ref[head_rows(h)].astype(jnp.float32)
            mix_ref[k, :, h * HEAD_SIZE : (h + 1) * HEAD_SIZE] = out.astype(jnp.bfloat16)

    halves = max(n for n in (1, 2, 4) if share % (n * 128) == 0)
    half = share // halves
    block = half

    def project(k, s, part):
        def body(n, carry):
            span = pl.ds(pl.multiple_of(part * half + n * block, 128), block)
            made = jnp.dot(
                mix_ref[k], w_ref[s, k * cols : (k + 1) * cols, span],
                preferred_element_type=jnp.float32,
            )
            acc_ref[s, :, span] = made if k == 0 else acc_ref[s, :, span] + made
            return carry

        lax.fori_loop(0, half // block, body, 0)

    def nothing(i):
        pass

    def new_token():
        both = pair_ref[...].astype(jnp.float32)
        which = lax.broadcasted_iota(jnp.int32, both.shape, 1)
        for kind in range(2):
            new_ref[kind] = jnp.sum(jnp.where(which == kind, both, 0.0), axis=1)
        for k in range(kv_heads):
            own_q(k).wait()
            new_key = new_ref[0, :, k * HEAD_SIZE : (k + 1) * HEAD_SIZE]
            lane = lax.broadcasted_iota(jnp.int32, (rows, LANES), 1)
            tile = jnp.zeros((rows, LANES), jnp.float32)
            for h in range(per_kv):
                q = q_ref[k, my_group, :, h * HEAD_SIZE : (h + 1) * HEAD_SIZE].astype(jnp.float32)
                tile = jnp.where(lane == h, jnp.sum(q * new_key, axis=1, keepdims=True) * SCALE, tile)
            new_st[k] = tile

    def kv_arrived(k):
        for kind in range(2):
            for copy in kv_all[k, kind][:-1]:
                copy.wait_recv()
            kv_all[k, kind][-1].wait()

    def whole(k, s):
        for part in range(halves):
            project(k, s, part)

    core = lax.rem(my_tp, 2)

    def hop(d, heads_of):
        if d < groups - 1:
            for k in heads_of:
                relay(k, d)

    hop(1, [0])
    lax.fori_loop(0, groups // 2, build, 0)
    hop(1, range(1, kv_heads))
    lax.fori_loop(groups // 2, groups, build, 0)
    to_smem.wait()
    new_token()

    reach = min(1, groups - 1)

    @pl.when(core == 0)
    def _():
        kv_arrived(0)
        attend_some(0, 0, reach)

    hop(2, [0])

    @pl.when(core == 1)
    def _():
        kv_arrived(0)
        attend_some(0, 0, reach)

    hop(2, range(1, kv_heads))
    for d in range(2, groups):
        if d > 2:
            hop(d, range(kv_heads))
        attend_some(0, d, d)

    def ahead(k):
        pass_on(k, nothing, nothing, far=False)

    def catch_up(k):
        kv_arrived(k)
        attend_some(k, 0, groups - 1, far=True)

    for k in range(1, kv_heads):

        @pl.when(core == 0)
        def _():
            catch_up(k)
            ahead(k - 1)

        @pl.when(core == 1)
        def _():
            ahead(k - 1)
            catch_up(k)

    for copy in w_copies:
        copy.wait()

    pass_on(chained, nothing, nothing)
    for k in range(chained):
        finish(k)
        for s in range(owners):
            whole(k, s)

    finish(chained)

    mate = {"tp": my_tp + 1 - 2 * lax.rem(my_tp, 2)}
    cores, fars = {}, {}

    def last(s, span):
        made = jnp.dot(
            mix_ref[chained], w_ref[s, chained * cols : (chained + 1) * cols, span],
            preferred_element_type=jnp.float32,
        )
        return made if chained == 0 else acc_ref[s, :, span] + made

    index = {(i, b): s for s, (i, b, _) in enumerate(slot_ids)}
    spans = [slice(p * half, (p + 1) * half) for p in range(halves)]
    for i in range(pairs):
        for p, span in enumerate(spans):
            cores[i, p] = remote(
                core_send.at[i, :, span], core_got.at[i, :, span],
                out_send.at[0, i, p], out_recv.at[0, i, p], mate,
            )
            if i > 0:
                fars[i, p] = remote(
                    far_send.at[i - 1, :, span], far_got.at[i - 1, :, span],
                    out_send.at[1, i, p], out_recv.at[1, i, p], {"tp": slot_ids[index[i, 0]][2]},
                )

    def to_mate(i, p):
        span = spans[p]
        core_send[i, :, span] = last(index[i, 1], span).astype(jnp.bfloat16)
        cores[i, p].start()

    def to_far(i, p):
        span = spans[p]
        made = last(index[i, 0], span)
        if i == 0:
            acc_ref[index[0, 0], :, span] = made
        else:
            cores[i, p].wait_recv()
            far_send[i - 1, :, span] = (
                made + core_got[i, :, span].astype(jnp.float32)
            ).astype(jnp.bfloat16)
            fars[i, p].start()

    @pl.when(core == 0)
    def _():
        for i in list(range(1, pairs)) + [0]:
            for p in range(halves):
                to_mate(i, p)
        for i in list(range(1, pairs)) + [0]:
            for p in range(halves):
                to_far(i, p)

    @pl.when(core == 1)
    def _():
        for i in list(range(1, pairs)) + [0]:
            for p in range(halves):
                to_far(i, p)
                to_mate(i, p)

    for p, span in enumerate(spans):
        cores[0, p].wait_recv()
        total = acc_ref[index[0, 0], :, span] + core_got[0, :, span].astype(jnp.float32)
        for i in range(1, pairs):
            fars[i, p].wait_recv()
            total = total + far_got[i - 1, :, span].astype(jnp.float32)
        out_ref[:, span] = total.astype(jnp.bfloat16)

    sent = small + list(cores.values()) + list(fars.values())
    for copies in kv_all.values():
        sent += copies[:-1]
    for copy in sent:
        copy.wait_send()
    for k in range(kv_heads):
        for d in range(1, groups):
            for way in (RIGHT, LEFT):
                source = q_cols(k) if d == 1 else None
                pl.when(can_send(way, d))(lambda: q_hop(k, way, d, source).wait_send())
    for k in range(kv_heads):
        for g in range(groups):

            @pl.when(my_group != g)
            def _():
                for copy in to_mid(k, g):
                    copy.wait_send()


def per_device(
    queries, newest_key_value, kv_pages, fetch_slots, block_table, prefix_len, out_weight
):
    T = lax.axis_size("tp")
    G = lax.axis_size("grp")
    rows, cols = queries.shape
    heads = cols // HEAD_SIZE
    kv_dev = max(1, heads // GROUP_WIDTH)
    per_kv = heads // kv_dev
    width = kv_dev * HEAD_SIZE
    pages_dev, _, page, _ = kv_pages.shape
    list_len = block_table.shape[1]
    limit = fetch_slots.shape[2]
    model = out_weight.shape[1]
    dma = pltpu.SemaphoreType.DMA

    share = model // T
    pairs = T // 2
    bf16, f32, i32 = jnp.bfloat16, jnp.float32, jnp.int32
    vmem = pltpu.VMEM
    h_pad = -(-per_kv // 8) * 8
    m_pad = -(-(list_len + 1) // 8) * 8
    tokens = T * limit * page
    part = (per_kv * rows, HEAD_SIZE)
    return pl.pallas_call(
        functools.partial(step_kernel, limit),
        out_shape=jax.ShapeDtypeStruct((rows, share), bf16),
        in_specs=[ANY_SPEC] * 7,
        out_specs=VMEM_SPEC,
        scratch_shapes=[
            vmem((list_len, rows), i32),
            vmem((1, rows), i32),
            vmem((limit, G), i32),
            vmem((rows, 2, width), bf16),
            vmem((2, rows, width), f32),
            vmem((kv_dev, G, rows, per_kv * HEAD_SIZE), bf16),
            vmem((G, m_pad, LANES), f32),
            vmem((T, 8, LANES), i32),
            pltpu.SMEM((T, 8, LANES), i32),
            vmem((G, rows, tokens), f32),
            vmem((tokens, HEAD_SIZE), bf16),
            vmem((tokens, 2 * HEAD_SIZE), bf16),
            vmem((kv_dev, G, *part), f32),
            vmem((kv_dev, G, rows, LANES), f32),
            vmem((kv_dev, G, *part), bf16),
            vmem((kv_dev, G, h_pad, LANES), f32),
            vmem((kv_dev, G, *part), bf16),
            vmem((kv_dev, G, h_pad, LANES), f32),
            vmem((kv_dev, G // 2, *part), bf16),
            vmem((kv_dev, G // 2, h_pad, LANES), f32),
            vmem((kv_dev, rows, LANES), f32),
            vmem((T, out_weight.shape[0], share), bf16),
            vmem((kv_dev, rows, per_kv * HEAD_SIZE), bf16),
            vmem((T, rows, share), f32),
            vmem((pairs, rows, share), bf16),
            vmem((pairs, rows, share), bf16),
            vmem((max(1, pairs - 1), rows, share), bf16),
            vmem((max(1, pairs - 1), rows, share), bf16),
            dma((T + G - 2,)),
            dma((T + G - 2,)),
            dma((2 * kv_dev, T - 1)),
            dma((2 * kv_dev, T - 1)),
            dma((kv_dev, 2, G - 1)),
            dma((kv_dev, 2, G - 1)),
            dma((kv_dev, G, 2)),
            dma((kv_dev, G, 2)),
            dma((kv_dev, G // 2, 2)),
            dma((2, pairs, 4)),
            dma((2, pairs, 4)),
            dma((3 * kv_dev + 5,)),
            dma((T,)),
        ]
        + [vmem((T, pages_dev, page, HEAD_SIZE), bf16)] * (2 * kv_dev),
        compiler_params=pltpu.CompilerParams(
            collective_id=0, has_side_effects=True, vmem_limit_bytes=VMEM_LIMIT
        ),
        name="decode_step",
    )(
        queries, kv_pages, block_table.T, prefix_len.reshape(1, rows),
        fetch_slots.reshape(G, limit).T, newest_key_value, out_weight,
    )


def solution(mesh):
    in_specs = (
        P(("rep", "grp"), "tp"),
        P(("rep", "grp"), None, None),
        P(("rep", "grp", "tp"), None, None, None),
        P("rep", ("grp", "tp"), None),
        P(("rep", "grp"), None),
        P(("rep", "grp")),
        P("tp", None),
    )
    out_specs = P(("rep", "grp"), "tp")
    return jax.shard_map(
        per_device, mesh=mesh, in_specs=in_specs, out_specs=out_specs, check_vma=False
    )
```
